32 devices in a mesh: grp: 2 (over y), chan: 4 (over z), stn: 2 (over x), pol: 2 (over core).
Axes of the slice: x: 2, y: 2, z: 4, core: 2. Of those that a mesh axis runs over, the one named last changes fastest.
Arguments:
- voltages: bfloat16 [4, 256, 16384], P(('grp', 'pol'), 'stn', 'chan'), parts along dimension 0, may hold values from -6 to 6
- fir_coeffs: float32 [16, 4096], replicated, may hold values from -1.5 to 1.5
- flags: int32 [4, 256], P(('grp', 'pol'), 'stn'), parts along dimension 0, may hold values 0 or 1
- station_slot: int32 [256], replicated, may hold values from 0 to 255, each once
- chan_map: int32 [2048], replicated, may hold values from 0 to 2047, each once
Outputs:
- visibilities: float32 [4, 256, 2, 256, 2, 256], P('grp', ('chan', 'stn'), 'pol'), parts along dimension 0
The draws below stay inside these ranges and needn't reach their ends.
There are 2 independent parts, one for each index of `grp`. The reference program is written for one: setup_inputs(seed, part) draws one part's arguments, and reference() takes and returns one part's arrays. A program takes and returns all parts, laid end to end along the dimension named above; an argument that names none is the same for every part. Nothing has to cross between parts.
Inputs may be any that keep to these rules, and one draw needn't show every extreme that they name: A permutation: station a's voltages are in row station_slot[a]. `chan_map`: a permutation of the 2048 channels.
All inputs are finite; a program needn't handle non-finite values. No bound on the sum of `flags` on one device may be relied on, other than what follows from the above.
Results may differ from the reference program's by a relative error of at most 0.0033.
Values may be sent and summed in bfloat16 or wider, within the bound.
No kernel may reach another device: no remote copies, remote signals or barrier semaphores. Data moves between devices by JAX's collectives and lax.ppermute only.
A program may use at most 128 MiB of HBM per device.

```python
import jax
import jax.numpy as jnp
from jax import lax

STATIONS = 256
POLS = 2
TAPS = 16
FL = 4096
CH = 2048
COARSE = 8
OUT_CH = 256
SAMPLES = 16384


def with_ends(array, key, low, top_value):
    index_at = [jax.random.randint(jax.random.fold_in(key, axis), (), 0, length) for axis, length in enumerate(array.shape)]
    longest = array.shape.index(max(array.shape))
    neighbour = index_at[:longest] + [(index_at[longest] + 1) % array.shape[longest]] + index_at[longest + 1:]
    return array.at[tuple(index_at)].set(low).at[tuple(neighbour)].set(top_value)


def steps_of(own_key, extent, cuts, smallest, high):
    def one(position, parts):
        steps = jax.random.uniform(jax.random.fold_in(jax.random.fold_in(own_key, 6), position), (parts,), jnp.float32, smallest / len(cuts), high / len(cuts))
        return jnp.repeat(jnp.exp(steps), extent[position] // parts).reshape((-1,) + (1,) * (len(extent) - position - 1))

    gain = one(*cuts[0])
    for cut in cuts[1:]:
        gain = gain * one(*cut)
    return gain


def gaussian(key, extent, width, limit, split=(), held_as=jnp.bfloat16):
    entries = jax.random.normal(key, extent, jnp.float32) * width
    if len(split) > 0:
        entries = steps_of(key, extent, split, -0.22, 0.18) * entries
    return jnp.clip(entries, min=-limit, max=limit).astype(held_as)


def setup_inputs(seed: int = 0, part: int = 0) -> dict:
    key_list = jax.random.split(jax.random.key(seed), 6)
    own_keys = jax.random.split(jax.random.fold_in(key_list[5], part), 6)
    voltages = gaussian(own_keys[0], (POLS, STATIONS, SAMPLES), 1.0, 6.0, ((0, 2), (1, 2), (2, 4)))
    fir_coeffs = gaussian(key_list[1], (TAPS, FL), TAPS ** -0.5, 1.5, (), jnp.float32)
    flags = with_ends((jax.random.randint(own_keys[2], (POLS, STATIONS), 0, 8) < 7).astype(jnp.int32), jax.random.fold_in(own_keys[2], 1), 0, 1)
    station_slot = jax.random.permutation(key_list[3], STATIONS).astype(jnp.int32)
    chan_map = jax.random.permutation(key_list[4], CH).astype(jnp.int32)
    return {"voltages": voltages, "fir_coeffs": fir_coeffs, "flags": flags, "station_slot": station_slot, "chan_map": chan_map}


def filter_one(row, flag, fir_coeffs, chan_map):
    frames_all = row.shape[0] // FL
    signal = row.astype(jnp.float32).reshape(frames_all, FL)
    padded = jnp.concatenate([jnp.zeros((TAPS - 1, FL), jnp.float32), signal], axis=0)
    filtered = jnp.zeros((frames_all, FL), jnp.float32)
    for tap_index in range(TAPS):
        filtered = filtered + fir_coeffs[tap_index] * padded[tap_index:tap_index + frames_all]
    spectrum = jnp.fft.rfft(filtered, axis=-1)[:, :CH]
    spectrum = jnp.take(spectrum, chan_map, axis=1) * (flag * FL ** -0.5)
    return jnp.real(spectrum).astype(jnp.bfloat16), jnp.imag(spectrum).astype(jnp.bfloat16)


def reference(voltages, fir_coeffs, flags, station_slot, chan_map):
    inputs = POLS * STATIONS
    rows_all = voltages.reshape(inputs, -1)
    flag_rows = flags.reshape(-1).astype(jnp.float32)
    frames_all = rows_all.shape[1] // FL

    def one_input(pair):
        return filter_one(pair[0], pair[1], fir_coeffs, chan_map)

    spec_re, spec_im = lax.map(one_input, (rows_all, flag_rows))
    order = jnp.concatenate([station_slot + pol_index * STATIONS for pol_index in range(POLS)]).astype(jnp.int32)
    spec_re = jnp.take(spec_re, order, axis=0)
    spec_im = jnp.take(spec_im, order, axis=0)
    scale = 1.0 / (frames_all * COARSE)

    def one_coarse(coarse_index):
        start = (coarse_index * COARSE).astype(jnp.int32)
        left_re = lax.dynamic_slice_in_dim(spec_re, start, COARSE, 2).reshape(inputs, -1)
        left_im = lax.dynamic_slice_in_dim(spec_im, start, COARSE, 2).reshape(inputs, -1)
        real_part = jnp.dot(left_re, left_re.T, preferred_element_type=jnp.float32) + jnp.dot(left_im, left_im.T, preferred_element_type=jnp.float32)
        imag_part = jnp.dot(left_im, left_re.T, preferred_element_type=jnp.float32) - jnp.dot(left_re, left_im.T, preferred_element_type=jnp.float32)
        return jnp.stack([real_part, imag_part]) * scale

    gram = lax.map(one_coarse, jnp.arange(OUT_CH, dtype=jnp.int32))
    gram = jnp.moveaxis(gram, 0, 1)
    return gram.reshape(2, OUT_CH, POLS, STATIONS, POLS, STATIONS)
```

```python
import functools
import math

import jax
import jax.numpy as jnp
import numpy as np
from jax import lax
from jax.experimental import pallas as pl
from jax.experimental.pallas import tpu as pltpu
from jax.sharding import PartitionSpec as P

TAPS = 16
FL = 4096
CH = 2048
COARSE = 8
RAD = 16
PT = FL // RAD
HALF = PT // 2
LANES = 128

f32 = jnp.float32
bf16 = jnp.bfloat16


def onehot(rows, cols):
    return (rows[:, None] == cols[None, :]).astype(bf16)


@functools.cache
def tables():
    p = np.arange(PT)[:, None]
    wide = []
    for c in range(1, RAD // 2):
        k2 = np.concatenate([np.arange(HALF), PT - 1 - np.arange(HALF)])[None, :]
        phase = (p * (c + RAD * k2) % FL) * (2.0 * math.pi / FL)
        wide.append(np.concatenate([np.cos(phase), -np.sin(phase)], axis=1))
    slim = []
    for c in (0, RAD // 2):
        k2 = np.arange(HALF)[None, :]
        phase = (p * (c + RAD * k2) % FL) * (2.0 * math.pi / FL)
        slim.append(np.concatenate([np.cos(phase), -np.sin(phase)], axis=1))
    out = []
    for table in (np.stack(wide), np.stack(slim)):
        table = table * FL**-0.5
        high = table.astype(np.float32).astype(jnp.bfloat16)
        low = (table - high.astype(np.float64)).astype(np.float32).astype(jnp.bfloat16)
        out += [high, low]
    return out


def real_dft16(x):
    def dft4(a0, a1, a2, a3):
        s02, d02, s13, d13 = a0 + a2, a0 - a2, a1 + a3, a1 - a3
        return s02 + s13, d02, -d13, s02 - s13

    cols = [dft4(x[b], x[4 + b], x[8 + b], x[12 + b]) for b in range(4)]
    out = [None] * 9
    r0, r1, i1, r2 = dft4(*(cols[b][0] for b in range(4)))
    out[0], out[4], out[8] = (r0, None), (r1, i1), (r2, None)
    h = math.sqrt(0.5)
    v0, v1, v2, v3 = (cols[b][3] for b in range(4))
    pr, pi = h * (v1 - v3), -h * (v1 + v3)
    out[2] = (v0 + pr, pi - v2)
    out[6] = (v0 - pr, v2 + pi)
    c1, s1 = math.cos(math.pi / 8), math.sin(math.pi / 8)
    re0, im0 = cols[0][1], cols[0][2]
    re1 = cols[1][1] * c1 + cols[1][2] * s1
    im1 = cols[1][2] * c1 - cols[1][1] * s1
    re2 = (cols[2][1] + cols[2][2]) * h
    im2 = (cols[2][2] - cols[2][1]) * h
    re3 = cols[3][1] * s1 + cols[3][2] * c1
    im3 = cols[3][2] * s1 - cols[3][1] * c1
    ar, ai, br, bi = re0 + re2, im0 + im2, re0 - re2, im0 - im2
    cr, ci, dr, di = re1 + re3, im1 + im3, re1 - re3, im1 - im3
    out[1] = (ar + cr, ai + ci)
    out[5] = (br + di, bi - dr)
    out[7] = (ar - cr, ci - ai)
    out[3] = (br - di, -bi - dr)
    return out


def split(value):
    high = value.astype(bf16)
    return high, (value - high.astype(f32)).astype(bf16)


def filterbank_kernel(frames, where_ref, *refs):
    blocks = refs[:frames]
    fir, flag, wide_hi, wide_lo, slim_hi, slim_lo, select = refs[frames : frames + 7]
    outs = refs[frames + 7 : -4]
    x, u_hi, u_lo, spec = refs[-4:]
    rows = blocks[0].shape[0]
    total = frames * rows
    for d in range(frames):
        x[pl.ds(where_ref[d], 1)] = blocks[d][...][None]
    step = 16
    for f in range(frames):
        for half in range(PT // LANES):

            def unit(i, carry, f=f, half=half):
                at = pl.multiple_of(i * step, step)
                keep = flag[pl.ds(at, step), :]
                filtered = []
                for q in range(RAD):
                    lanes = slice(PT * q + LANES * half, PT * q + LANES * (half + 1))
                    acc = None
                    for lag in range(f + 1):
                        term = fir[TAPS - 1 - lag, lanes][None, :] * x[f - lag, pl.ds(at, step), lanes].astype(f32)
                        acc = term if acc is None else acc + term
                    filtered.append(acc * keep)
                parts = []
                for re, im in real_dft16(filtered):
                    parts += [re] if im is None else [re, im]
                for n, part in enumerate(parts):
                    high, low = split(part)
                    to = (n, pl.ds(pl.multiple_of(f * rows + at, step), step), slice(LANES * half, LANES * (half + 1)))
                    u_hi[to] = high
                    u_lo[to] = low
                return carry

            lax.fori_loop(0, rows // step, unit, 0)

    def three(first, count, hi, lo):
        a = u_hi[first : first + count].reshape(count * total, PT)
        b = u_lo[first : first + count].reshape(count * total, PT)
        out = jnp.dot(a, hi, preferred_element_type=f32)
        out = out + jnp.dot(b, hi, preferred_element_type=f32)
        return out + jnp.dot(a, lo, preferred_element_type=f32)

    for n, c in enumerate((0, RAD // 2)):
        got = three(0 if c == 0 else RAD - 1, 1, slim_hi[n], slim_lo[n])
        spec[:total, c * HALF : (c + 1) * HALF] = got[:, :HALF].astype(bf16)
        spec[total:, c * HALF : (c + 1) * HALF] = got[:, HALF:].astype(bf16)
    for c in range(1, RAD // 2):
        got = three(2 * c - 1, 2, wide_hi[c - 1], wide_lo[c - 1])
        re = got[:total, :PT] - got[total:, PT:]
        im = got[:total, PT:] + got[total:, :PT]
        o = RAD - c
        spec[:total, c * HALF : (c + 1) * HALF] = re[:, :HALF].astype(bf16)
        spec[total:, c * HALF : (c + 1) * HALF] = im[:, :HALF].astype(bf16)
        spec[:total, o * HALF : (o + 1) * HALF] = re[:, HALF:].astype(bf16)
        spec[total:, o * HALF : (o + 1) * HALF] = (-im[:, HALF:]).astype(bf16)
    slots = outs[0].shape[0]
    for d, out in enumerate(outs):
        out[...] = lax.dot_general(
            select[d * slots : (d + 1) * slots, :], spec[...], (((1,), (1,)), ((), ())), preferred_element_type=f32
        ).astype(bf16)


def filterbank(where, blocks, fir, flag, select, pieces, slots):
    frames, rows = len(blocks), blocks[0].shape[0]
    total = frames * rows
    vmem = pl.BlockSpec(memory_space=pltpu.VMEM)
    consts = [jnp.asarray(t) for t in tables()]
    return pl.pallas_call(
        functools.partial(filterbank_kernel, frames),
        out_shape=[jax.ShapeDtypeStruct((slots, 2 * total), bf16)] * pieces,
        in_specs=[pl.BlockSpec(memory_space=pltpu.SMEM)] + [vmem] * (frames + 7),
        out_specs=[vmem] * pieces,
        scratch_shapes=[
            pltpu.VMEM((frames, rows, FL), bf16),
            pltpu.VMEM((RAD, total, PT), bf16),
            pltpu.VMEM((RAD, total, PT), bf16),
            pltpu.VMEM((2 * total, CH), bf16),
        ],
        compiler_params=pltpu.CompilerParams(vmem_limit_bytes=48 << 20),
        name="filterbank",
    )(where, *blocks, fir, flag, *consts, select)


def order_kernel(pieces, *refs):
    place, out, turned = refs[pieces:]
    half = refs[0].shape[1] // 2
    slots = refs[0].shape[0]
    parts = []
    for part in range(2):
        rows = jnp.concatenate([refs[d][:, part * half : (part + 1) * half] for d in range(pieces)], axis=1)
        got = jnp.dot(rows, place[...], preferred_element_type=f32)
        parts.append(got.reshape(slots // COARSE, 1, COARSE, got.shape[1]))
    re, im = parts
    shape = (2 * slots, re.shape[3])
    out[...] = jnp.concatenate([re, im], axis=1).reshape(shape).astype(bf16)
    turned[...] = jnp.concatenate([im, -re], axis=1).reshape(shape).astype(bf16)


def order(blocks, place):
    slots = blocks[0].shape[0]
    vmem = pl.BlockSpec(memory_space=pltpu.VMEM)
    shape = jax.ShapeDtypeStruct((2 * slots, place.shape[1]), bf16)
    return pl.pallas_call(
        functools.partial(order_kernel, len(blocks)),
        out_shape=[shape, shape],
        in_specs=[vmem] * (len(blocks) + 1),
        out_specs=[vmem] * 2,
        compiler_params=pltpu.CompilerParams(vmem_limit_bytes=40 << 20),
        name="order",
    )(*blocks, place)


def gram_kernel(frames, scale, pol_ref, own, turned, other, out):
    stations = own.shape[1] // frames
    first = pol_ref[0] == 0
    turns = (((0,), (0,)), ((), ()))
    for j in range(own.shape[0] // (2 * COARSE)):

        def stack(ref):
            rows = slice(2 * COARSE * j, 2 * COARSE * (j + 1))
            return jnp.concatenate([ref[rows, f * stations : (f + 1) * stations] for f in range(frames)], axis=0)

        mine, mine_turned, theirs = stack(own), stack(turned), stack(other)
        right = jnp.concatenate([jnp.where(first, mine, theirs), jnp.where(first, theirs, mine)], axis=1)
        for part, left in enumerate((mine, mine_turned)):
            got = lax.dot_general(left, right, turns, preferred_element_type=f32) * scale
            tiles = stations // LANES
            for q in range(2):
                for t in range(tiles):
                    at = q * stations + t * LANES
                    out[part, j, pl.ds(2 * t + q, stations, stride=2 * tiles), :] = got[:, at : at + LANES]


def gram(pol, own, turned, other, frames):
    coarse = own.shape[0] // (2 * COARSE)
    stations = own.shape[1] // frames
    tiles = stations // LANES
    per = 2
    rows = pl.BlockSpec((per * 2 * COARSE, own.shape[1]), lambda i: (i, 0))
    return pl.pallas_call(
        functools.partial(gram_kernel, frames, 1.0 / (frames * COARSE)),
        grid=(coarse // per,),
        out_shape=jax.ShapeDtypeStruct((2, coarse, stations * 2 * tiles, LANES), f32),
        in_specs=[pl.BlockSpec(memory_space=pltpu.SMEM), rows, rows, rows],
        out_specs=pl.BlockSpec((2, per, stations * 2 * tiles, LANES), lambda i: (0, i, 0, 0)),
        compiler_params=pltpu.CompilerParams(vmem_limit_bytes=40 << 20),
        name="gram",
    )(pol, own, turned, other)


def rolled(array, axis, start, size):
    return lax.dynamic_slice_in_dim(jnp.concatenate([array, array], axis=axis), start, size, axis=axis)


def fast_body(voltages, fir_coeffs, flags, station_slot, chan_map):
    chans, stns = lax.axis_size("chan"), lax.axis_size("stn")
    chan, stn, pol = lax.axis_index("chan"), lax.axis_index("stn"), lax.axis_index("pol")
    here = voltages.shape[1]
    stations = station_slot.shape[0]
    frames = chans
    rows = here // chans
    owners = chans * stns
    slots = CH // owners
    shares = voltages.reshape(chans, rows, FL)
    blocks = [lax.dynamic_index_in_dim(shares, chan, 0, keepdims=False)]
    for d in range(1, chans):
        share = lax.dynamic_index_in_dim(shares, (chan + d) % chans, 0, keepdims=False)
        blocks.append(lax.ppermute(share, "chan", [(i, (i + d) % chans) for i in range(chans)]))
    where = (chan - jnp.arange(chans, dtype=jnp.int32)) % chans
    keep = lax.dynamic_slice_in_dim(flags[0], chan * rows, rows).astype(f32)
    keep = jnp.broadcast_to(keep[:, None], (rows, LANES))
    lane_of = (chan_map % RAD) * HALF + chan_map // RAD
    lane_of = rolled(rolled(lane_of.reshape(chans, stns, slots), 0, chan, chans), 1, stn, stns)
    select = onehot(lane_of.reshape(CH), jnp.arange(CH, dtype=jnp.int32))
    pieces = filterbank(where, blocks, fir_coeffs, keep, select, owners, slots)
    got = []
    for d in range(owners):
        dc, ds = divmod(d, stns)
        if d == 0:
            got.append(pieces[0])
            continue
        route = [
            (i * stns + j, (i + dc) % chans * stns + (j + ds) % stns) for i in range(chans) for j in range(stns)
        ]
        got.append(lax.ppermute(pieces[d], ("chan", "stn"), route))
    dist = jnp.arange(owners, dtype=jnp.int32)
    row0 = (stn - dist % stns) % stns * here + (chan - dist // stns) % chans * rows
    row = row0[:, None, None] + jnp.arange(rows, dtype=jnp.int32)[None, None, :]
    row = row + stations * jnp.arange(frames, dtype=jnp.int32)[None, :, None]
    col = station_slot[None, :] + stations * jnp.arange(frames, dtype=jnp.int32)[:, None]
    place = onehot(row.reshape(-1), col.reshape(-1))
    own, turned = order(got, place)
    other = lax.ppermute(own, "pol", [(0, 1), (1, 0)])
    out = gram(pol.reshape(1), own, turned, other, frames)
    tiles = stations // LANES
    out = out.reshape(2, -1, stations, tiles, 2, LANES).transpose(0, 1, 2, 4, 3, 5)
    return out.reshape(2, -1, 1, stations, 2, stations)


def general_body(voltages, fir_coeffs, flags, station_slot, chan_map):
    high = lax.Precision.HIGHEST
    here = voltages.shape[1]
    chans, stns = lax.axis_size("chan"), lax.axis_size("stn")
    frames_here = voltages.shape[2] // FL
    frames = voltages.reshape(here, frames_here, FL)
    history = []
    for distance in range(1, (TAPS - 1 + frames_here - 1) // frames_here + 1):
        route = [(i - distance, i) for i in range(distance, chans)]
        history = [lax.ppermute(frames, "chan", route)] + history
    window = jnp.concatenate(history + [frames], axis=1)
    window = window[:, window.shape[1] - frames_here - TAPS + 1 :]
    filtered = jnp.zeros((here, frames_here, FL), f32)
    for tap in range(TAPS):
        filtered = filtered + fir_coeffs[tap][None, None, :] * window[:, tap : tap + frames_here, :].astype(f32)
    side = math.isqrt(FL)

    def angles(rows, cols, period):
        product = jnp.arange(rows, dtype=jnp.int32)[:, None] * jnp.arange(cols, dtype=jnp.int32)[None, :]
        phase = (product % period).astype(f32) * (2.0 * math.pi / period)
        return jnp.cos(phase), jnp.sin(phase)

    grid = filtered.reshape(here, frames_here, side, side)
    cos, sin = angles(side, side, side)
    re = jnp.einsum("sfqp,qc->sfpc", grid, cos, precision=high)
    im = -jnp.einsum("sfqp,qc->sfpc", grid, sin, precision=high)
    cos, sin = angles(side, side, FL)
    re, im = re * cos + im * sin, im * cos - re * sin
    cos, sin = angles(side, side // 2, side)
    form = "sfpc,pk->kcfs"
    out_re = jnp.einsum(form, re, cos, precision=high) + jnp.einsum(form, im, sin, precision=high)
    out_im = jnp.einsum(form, im, cos, precision=high) - jnp.einsum(form, re, sin, precision=high)
    weight = jnp.tile(flags[0].astype(f32), frames_here) * FL**-0.5
    shape = (CH, 1, frames_here * here)
    spectra = jnp.concatenate(
        [(out_re.reshape(shape) * weight).astype(bf16), (out_im.reshape(shape) * weight).astype(bf16)], axis=1
    )
    select = onehot(chan_map, jnp.arange(CH, dtype=jnp.int32))
    spectra = jnp.einsum("sc,cpn->spn", select, spectra, preferred_element_type=f32).astype(bf16)
    pieces = lax.all_to_all(spectra, ("chan", "stn"), split_axis=0, concat_axis=2, tiled=True)
    pieces = pieces.reshape(-1, 2, chans, stns, frames_here, here).transpose(0, 1, 3, 5, 2, 4)
    total = chans * frames_here
    pieces = pieces.reshape(-1, COARSE, 2, stns * here, total)
    place = onehot(station_slot, jnp.arange(stns * here, dtype=jnp.int32))
    own = jnp.einsum("ar,jkprf->jkpaf", place, pieces, preferred_element_type=f32).astype(bf16)
    both = lax.all_gather(own[None], "pol", axis=0, tiled=True)
    form = "jkrf,qjksf->jrqs"

    def dot(left, right):
        return jnp.einsum(form, left, right, preferred_element_type=f32)

    own_re, own_im, re, im = own[:, :, 0], own[:, :, 1], both[:, :, :, 0], both[:, :, :, 1]
    block = jnp.stack([dot(own_re, re) + dot(own_im, im), dot(own_im, re) - dot(own_re, im)], axis=0)
    return (block * (1.0 / (total * COARSE)))[:, :, None]


def body(voltages, fir_coeffs, flags, station_slot, chan_map):
    chans, stns = lax.axis_size("chan"), lax.axis_size("stn")
    here, stations = voltages.shape[1], station_slot.shape[0]
    fits = (
        voltages.shape[2] == FL
        and chans <= TAPS
        and here % chans == 0
        and here // chans % 16 == 0
        and here % LANES == 0
        and stations % LANES == 0
        and CH // (chans * stns) % 16 == 0
    )
    return (fast_body if fits else general_body)(voltages, fir_coeffs, flags, station_slot, chan_map)


def solution(mesh):
    in_specs = (P(("grp", "pol"), "stn", "chan"), P(), P(("grp", "pol"), "stn"), P(), P())
    out_specs = P("grp", ("chan", "stn"), "pol", None, None, None)
    return jax.shard_map(body, mesh=mesh, in_specs=in_specs, out_specs=out_specs, check_vma=False)
```

```python
import functools
import math

import jax
import jax.numpy as jnp
import numpy as np
from jax import lax
from jax.experimental import pallas as pl
from jax.experimental.pallas import tpu as pltpu
from jax.sharding import PartitionSpec as P

TAPS = 16
FL = 4096
CH = 2048
COARSE = 8
RAD = 16
PT = FL // RAD
HALF = PT // 2
LANES = 128
BATCH = 4

f32 = jnp.float32
bf16 = jnp.bfloat16


def onehot(rows, cols):
    return (rows[:, None] == cols[None, :]).astype(bf16)


@functools.cache
def tables():
    p = np.arange(PT)[None, :]
    rows = []
    for k2 in (np.arange(HALF), PT - 1 - np.arange(HALF)):
        phase = (k2[:, None] * p % PT) * (2.0 * math.pi / PT)
        rows += [np.cos(phase), -np.sin(phase)]
    table = np.concatenate(rows) * FL**-0.5
    high = table.astype(np.float32).astype(jnp.bfloat16)
    low = (table - high.astype(np.float64)).astype(np.float32).astype(jnp.bfloat16)
    phase = np.arange(1, RAD // 2 + 1)[:, None] * p * (2.0 * math.pi / FL)
    twiddle = np.concatenate([np.cos(phase), np.sin(phase)]).astype(np.float32)
    return high, low, twiddle


def real_dft16(x):
    def dft4(a0, a1, a2, a3):
        s02, d02, s13, d13 = a0 + a2, a0 - a2, a1 + a3, a1 - a3
        return s02 + s13, d02, -d13, s02 - s13

    cols = [dft4(x[b], x[4 + b], x[8 + b], x[12 + b]) for b in range(4)]
    out = [None] * 9
    r0, r1, i1, r2 = dft4(*(cols[b][0] for b in range(4)))
    out[0], out[4], out[8] = (r0, None), (r1, i1), (r2, None)
    h = math.sqrt(0.5)
    v0, v1, v2, v3 = (cols[b][3] for b in range(4))
    pr, pi = h * (v1 - v3), -h * (v1 + v3)
    out[2] = (v0 + pr, pi - v2)
    out[6] = (v0 - pr, v2 + pi)
    c1, s1 = math.cos(math.pi / 8), math.sin(math.pi / 8)
    re0, im0 = cols[0][1], cols[0][2]
    re1 = cols[1][1] * c1 + cols[1][2] * s1
    im1 = cols[1][2] * c1 - cols[1][1] * s1
    re2 = (cols[2][1] + cols[2][2]) * h
    im2 = (cols[2][2] - cols[2][1]) * h
    re3 = cols[3][1] * s1 + cols[3][2] * c1
    im3 = cols[3][2] * s1 - cols[3][1] * c1
    ar, ai, br, bi = re0 + re2, im0 + im2, re0 - re2, im0 - im2
    cr, ci, dr, di = re1 + re3, im1 + im3, re1 - re3, im1 - im3
    out[1] = (ar + cr, ai + ci)
    out[5] = (br + di, bi - dr)
    out[7] = (ar - cr, ci - ai)
    out[3] = (br - di, -bi - dr)
    return out


def split(value):
    high = value.astype(bf16)
    return high, (value - high.astype(f32)).astype(bf16)


def filterbank_kernel(frames, rows, offset, share, sizes, chan_ref, *refs):
    volts, *blocks = refs[:frames]
    fir_in, flag_in, twiddle_in, high_in, low_in, select_in = refs[frames : frames + 6]
    pieces = len(refs) - frames - 6 - 14
    outs = refs[frames + 6 : frames + 6 + pieces]
    x, fir, flag, twiddle, dft_hi, dft_lo, select, u_hi, u_lo, spec, ready, in_sems, load_sems, out_sems = refs[
        frames + 6 + pieces :
    ]
    total = frames * rows
    chan = chan_ref[0]
    begin = pl.multiple_of(chan * share + offset, rows)
    first = []
    for d in range(frames):
        source = volts.at[0, pl.ds(begin, rows)] if d == 0 else blocks[d - 1]
        first.append(pltpu.make_async_copy(source, x.at[lax.rem(chan + frames - d, frames)], in_sems.at[d]))
    for n, (source, to) in enumerate(((fir_in, fir), (flag_in, flag), (twiddle_in, twiddle))):
        first.append(pltpu.make_async_copy(source, to, in_sems.at[frames + n]))
    loads = [
        pltpu.make_async_copy(source, to, load_sems.at[n])
        for n, (source, to) in enumerate(((high_in, dft_hi), (low_in, dft_lo), (select_in, select)))
    ]
    for copy in first + loads:
        copy.start()
    for copy in first:
        copy.wait()
    step = 16
    halves = PT // LANES
    for f in range(frames):

        def unit(i, carry, f=f):
            at = pl.multiple_of(i // halves * step, step)
            base = pl.multiple_of(i % halves * LANES, LANES)
            filtered = []
            for q in range(RAD):
                lanes = pl.ds(pl.multiple_of(PT * q + base, LANES), LANES)
                acc = None
                for lag in range(f + 1):
                    tap = TAPS - 1 - lag
                    term = fir[tap : tap + 1, lanes] * x[f - lag, pl.ds(at, step), lanes].astype(f32)
                    acc = term if acc is None else acc + term
                filtered.append(acc)
            parts = []
            for c, (re, im) in enumerate(real_dft16(filtered)):
                if c == 0:
                    parts.append(re)
                    continue
                cos = twiddle[c - 1 : c, pl.ds(base, LANES)]
                sin = twiddle[RAD // 2 + c - 1 : RAD // 2 + c, pl.ds(base, LANES)]
                parts += [re * cos, -re * sin] if im is None else [re * cos + im * sin, im * cos - re * sin]
            for n, part in enumerate(parts):
                high, low = split(part)
                to = (n, pl.ds(pl.multiple_of(f * rows + at, step), step), pl.ds(base, LANES))
                u_hi[to] = high
                u_lo[to] = low
            return carry

        lax.fori_loop(0, rows // step * halves, unit, 0)
    for copy in loads[:2]:
        copy.wait()
    contract = (((1,), (1,)), ((), ()))

    def three(at, count, outputs):
        a = u_hi[pl.ds(at, count)].reshape(count * total, PT)
        b = u_lo[pl.ds(at, count)].reshape(count * total, PT)
        hi, lo = dft_hi[:outputs], dft_lo[:outputs]
        out = lax.dot_general(hi, a, contract, preferred_element_type=f32)
        out = out + lax.dot_general(hi, b, contract, preferred_element_type=f32)
        return out + lax.dot_general(lo, a, contract, preferred_element_type=f32)

    lane = lax.broadcasted_iota(jnp.int32, (1, flag.shape[1]), 1)
    mine = pltpu.roll(flag[...].astype(f32), lax.rem(2 * flag.shape[1] - begin, flag.shape[1]), 1)
    keep = mine
    for f in range(1, frames):
        keep = jnp.where(lane >= f * rows, pltpu.roll(mine, f * rows, 1), keep)
    keep = keep[:, :total]

    def put(c, re, im):
        spec[c, :, :total] = (re * keep).astype(bf16)
        spec[c, :, total:] = (im * keep).astype(bf16)

    def pair(c, carry):
        got = three(2 * c - 1, 2, 2 * PT)
        re, im = got[:, :total], got[:, total:]
        put(c, re[:HALF] - im[HALF:PT], re[HALF:PT] + im[:HALF])
        o = PT + HALF
        put(RAD - c, re[PT:o] - im[o:], -(re[o:] + im[PT:o]))
        return carry

    got = three(0, 1, PT)
    put(0, got[:HALF], got[HALF:])
    got = three(RAD - 1, 2, PT)
    re, im = got[:, :total], got[:, total:]
    put(RAD // 2, re[:HALF] - im[HALF:], re[HALF:] + im[:HALF])
    lax.fori_loop(1, RAD // 2, pair, 0, unroll=True)
    loads[2].wait()
    at = 0
    right = spec[...].reshape(CH, 2 * total)
    owners = pieces // len(sizes)
    copies = []
    for h, size in enumerate(sizes):
        batch = BATCH
        some = [
            pltpu.make_async_copy(
                ready.at[pl.ds(at + d * size, size)], outs[h * owners + d], out_sems.at[h * owners + d]
            )
            for d in range(owners)
        ]

        def piece(i, carry, at=at, size=size, batch=batch, some=some):
            rows_of = pl.ds(pl.multiple_of(at + i * (batch * size), size), batch * size)
            ready[rows_of, :] = jnp.dot(select[rows_of, :], right, preferred_element_type=f32).astype(bf16)
            for d, copy in enumerate(some):

                @pl.when(d // batch == i)
                def _(copy=copy):
                    copy.start()

            return carry

        lax.fori_loop(0, owners // batch, piece, 0)
        copies += some
        at += owners * size
    for copy in copies:
        copy.wait()


def filterbank(chan, volts, blocks, fir, flag, select, owners, sizes, offset, share):
    frames, rows = len(blocks) + 1, blocks[0].shape[0]
    total = frames * rows
    hbm = pl.BlockSpec(memory_space=pltpu.HBM)
    high, low, twiddle = (jnp.asarray(t) for t in tables())
    outs = [jax.ShapeDtypeStruct((size, 2 * total), bf16) for size in sizes for _ in range(owners)]
    got = pl.pallas_call(
        functools.partial(filterbank_kernel, frames, rows, offset, share, sizes),
        out_shape=outs,
        in_specs=[pl.BlockSpec(memory_space=pltpu.SMEM)] + [hbm] * (frames + 6),
        out_specs=[hbm] * len(outs),
        scratch_shapes=[
            pltpu.VMEM((frames, rows, FL), bf16),
            pltpu.VMEM(fir.shape, f32),
            pltpu.VMEM(flag.shape, flag.dtype),
            pltpu.VMEM(twiddle.shape, f32),
            pltpu.VMEM(high.shape, bf16),
            pltpu.VMEM(low.shape, bf16),
            pltpu.VMEM(select.shape, bf16),
            pltpu.VMEM((RAD + 1, total, PT), bf16),
            pltpu.VMEM((RAD + 1, total, PT), bf16),
            pltpu.VMEM((RAD, HALF, 2 * total), bf16),
            pltpu.VMEM((CH, 2 * total), bf16),
            pltpu.SemaphoreType.DMA((frames + 3,)),
            pltpu.SemaphoreType.DMA((3,)),
            pltpu.SemaphoreType.DMA((len(outs),)),
        ],
        compiler_params=pltpu.CompilerParams(vmem_limit_bytes=56 << 20),
        name="filterbank",
    )(chan, volts, *blocks, fir, flag, twiddle, high, low, select)
    return [got[h * owners : (h + 1) * owners] for h in range(len(sizes))]


def order_kernel(pieces, *refs):
    place, out, turned = refs[pieces:]
    half = refs[0].shape[1] // 2
    slots = refs[0].shape[0]
    parts = []
    for part in range(2):
        rows = jnp.concatenate([refs[d][:, part * half : (part + 1) * half] for d in range(pieces)], axis=1)
        got = jnp.dot(rows, place[...], preferred_element_type=f32)
        parts.append(got.reshape(slots // COARSE, 1, COARSE, got.shape[1]))
    re, im = parts
    shape = (2 * slots, re.shape[3])
    out[...] = jnp.concatenate([re, im], axis=1).reshape(shape).astype(bf16)
    turned[...] = jnp.concatenate([im, -re], axis=1).reshape(shape).astype(bf16)


def order(blocks, place):
    slots = blocks[0].shape[0]
    vmem = pl.BlockSpec(memory_space=pltpu.VMEM)
    shape = jax.ShapeDtypeStruct((2 * slots, place.shape[1]), bf16)
    return pl.pallas_call(
        functools.partial(order_kernel, len(blocks)),
        out_shape=[shape, shape],
        in_specs=[vmem] * (len(blocks) + 1),
        out_specs=[vmem] * 2,
        compiler_params=pltpu.CompilerParams(vmem_limit_bytes=16 << 20),
        name="order",
    )(*blocks, place)


def gram_kernel(frames, start, scale, pol_ref, own, turned, other, *refs):
    out, ring, sems = refs[-3:]
    stations = own.shape[1] // frames
    tiles = stations // LANES
    first = pol_ref[0] == 0
    turns = (((0,), (0,)), ((), ()))
    count = own.shape[0] // (2 * COARSE)
    depth = ring.shape[0]

    def copies(j):
        slot = lax.rem(j, depth)
        return [
            pltpu.make_async_copy(ring.at[slot, part], out.at[part, start + j], sems.at[slot, part])
            for part in range(2)
        ]

    def one(j, carry):
        slot = lax.rem(j, depth)

        @pl.when(j >= depth)
        def _():
            for copy in copies(j - depth):
                copy.wait()

        def stack(ref):
            rows = pl.ds(pl.multiple_of(2 * COARSE * j, 2 * COARSE), 2 * COARSE)
            return jnp.concatenate([ref[rows, f * stations : (f + 1) * stations] for f in range(frames)], axis=0)

        mine, mine_turned, theirs = stack(own), stack(turned), stack(other)
        right = jnp.concatenate([jnp.where(first, mine, theirs), jnp.where(first, theirs, mine)], axis=1)
        for part, left in enumerate((mine, mine_turned)):
            got = lax.dot_general(left, right, turns, preferred_element_type=f32) * scale
            for q in range(2):
                for t in range(tiles):
                    at = q * stations + t * LANES
                    ring[slot, part, pl.ds(2 * t + q, stations, stride=2 * tiles), :] = got[:, at : at + LANES]
        for copy in copies(j):
            copy.start()
        return carry

    lax.fori_loop(0, count, one, 0)
    for j in range(count - depth, count):
        for copy in copies(j):
            copy.wait()


def gram(pol, own, turned, other, frames, coarse, start, into):
    count = own.shape[0] // (2 * COARSE)
    stations = own.shape[1] // frames
    rows = stations * 2 * (stations // LANES)
    depth = min(4, count)
    vmem, hbm = pl.BlockSpec(memory_space=pltpu.VMEM), pl.BlockSpec(memory_space=pltpu.HBM)
    more = [] if into is None else [into]
    return pl.pallas_call(
        functools.partial(gram_kernel, frames, start, 1.0 / (frames * COARSE)),
        out_shape=jax.ShapeDtypeStruct((2, coarse, rows, LANES), f32),
        in_specs=[pl.BlockSpec(memory_space=pltpu.SMEM), vmem, vmem, vmem] + [hbm] * len(more),
        out_specs=hbm,
        scratch_shapes=[pltpu.VMEM((depth, 2, rows, LANES), f32), pltpu.SemaphoreType.DMA((depth, 2))],
        input_output_aliases={4: 0} if more else {},
        compiler_params=pltpu.CompilerParams(vmem_limit_bytes=16 << 20),
        name="gram",
    )(pol, own, turned, other, *more)


def rolled(array, axis, start, size):
    return lax.dynamic_slice_in_dim(jnp.concatenate([array, array], axis=axis), start, size, axis=axis)


def groups_of(rows):
    return [(0, rows)]


def fast_body(voltages, fir_coeffs, flags, station_slot, chan_map):
    chans, stns = lax.axis_size("chan"), lax.axis_size("stn")
    chan, stn, pol = lax.axis_index("chan"), lax.axis_index("stn"), lax.axis_index("pol")
    here = voltages.shape[1]
    stations = station_slot.shape[0]
    frames = chans
    rows = here // chans
    owners = chans * stns
    slots = CH // owners
    coarse = slots // COARSE
    groups = groups_of(rows)
    shares = voltages.reshape(chans, rows, FL)
    blocks = []
    for offset, size in groups:
        blocks.append([])
        for d in range(1, chans):
            share = lax.dynamic_index_in_dim(shares[:, offset : offset + size], (chan + d) % chans, 0, keepdims=False)
            blocks[-1].append(lax.ppermute(share, "chan", [(i, (i + d) % chans) for i in range(chans)]))
    lane_of = (chan_map % RAD) * HALF + chan_map // RAD
    lane_of = rolled(rolled(lane_of.reshape(chans, stns, slots), 0, chan, chans), 1, stn, stns)
    select = onehot(lane_of.reshape(CH), jnp.arange(CH, dtype=jnp.int32))
    got = []
    place = []
    dist = jnp.arange(owners, dtype=jnp.int32)
    row0 = (stn - dist % stns) % stns * here + (chan - dist // stns) % chans * rows
    col = station_slot[None, :] + stations * jnp.arange(frames, dtype=jnp.int32)[:, None]
    for (offset, size), block in zip(groups, blocks, strict=True):
        [pieces] = filterbank(
            chan.reshape(1), voltages, block, fir_coeffs, flags, select, owners, [slots], offset, rows
        )
        got.append(pieces[0])
        for d in range(1, owners):
            dc, ds = divmod(d, stns)
            route = [
                (i * stns + j, (i + dc) % chans * stns + (j + ds) % stns) for i in range(chans) for j in range(stns)
            ]
            got.append(lax.ppermute(pieces[d], ("chan", "stn"), route))
        row = row0[:, None, None] + offset + jnp.arange(size, dtype=jnp.int32)[None, None, :]
        row = row + stations * jnp.arange(frames, dtype=jnp.int32)[None, :, None]
        place.append(row.reshape(-1))
    place = onehot(jnp.concatenate(place), col.reshape(-1))
    own, turned = order(got, place)
    other = lax.ppermute(own, "pol", [(0, 1), (1, 0)])
    out = gram(pol.reshape(1), own, turned, other, frames, coarse, 0, None)
    tiles = stations // LANES
    out = out.reshape(2, -1, stations, tiles, 2, LANES).transpose(0, 1, 2, 4, 3, 5)
    return out.reshape(2, -1, 1, stations, 2, stations)


def general_body(voltages, fir_coeffs, flags, station_slot, chan_map):
    high = lax.Precision.HIGHEST
    here = voltages.shape[1]
    chans, stns = lax.axis_size("chan"), lax.axis_size("stn")
    frames_here = voltages.shape[2] // FL
    frames = voltages.reshape(here, frames_here, FL)
    history = []
    for distance in range(1, (TAPS - 1 + frames_here - 1) // frames_here + 1):
        route = [(i - distance, i) for i in range(distance, chans)]
        history = [lax.ppermute(frames, "chan", route)] + history
    window = jnp.concatenate(history + [frames], axis=1)
    window = window[:, window.shape[1] - frames_here - TAPS + 1 :]
    filtered = jnp.zeros((here, frames_here, FL), f32)
    for tap in range(TAPS):
        filtered = filtered + fir_coeffs[tap][None, None, :] * window[:, tap : tap + frames_here, :].astype(f32)
    side = math.isqrt(FL)

    def angles(rows, cols, period):
        product = jnp.arange(rows, dtype=jnp.int32)[:, None] * jnp.arange(cols, dtype=jnp.int32)[None, :]
        phase = (product % period).astype(f32) * (2.0 * math.pi / period)
        return jnp.cos(phase), jnp.sin(phase)

    grid = filtered.reshape(here, frames_here, side, side)
    cos, sin = angles(side, side, side)
    re = jnp.einsum("sfqp,qc->sfpc", grid, cos, precision=high)
    im = -jnp.einsum("sfqp,qc->sfpc", grid, sin, precision=high)
    cos, sin = angles(side, side, FL)
    re, im = re * cos + im * sin, im * cos - re * sin
    cos, sin = angles(side, side // 2, side)
    form = "sfpc,pk->kcfs"
    out_re = jnp.einsum(form, re, cos, precision=high) + jnp.einsum(form, im, sin, precision=high)
    out_im = jnp.einsum(form, im, cos, precision=high) - jnp.einsum(form, re, sin, precision=high)
    weight = jnp.tile(flags[0].astype(f32), frames_here) * FL**-0.5
    shape = (CH, 1, frames_here * here)
    spectra = jnp.concatenate(
        [(out_re.reshape(shape) * weight).astype(bf16), (out_im.reshape(shape) * weight).astype(bf16)], axis=1
    )
    select = onehot(chan_map, jnp.arange(CH, dtype=jnp.int32))
    spectra = jnp.einsum("sc,cpn->spn", select, spectra, preferred_element_type=f32).astype(bf16)
    pieces = lax.all_to_all(spectra, ("chan", "stn"), split_axis=0, concat_axis=2, tiled=True)
    pieces = pieces.reshape(-1, 2, chans, stns, frames_here, here).transpose(0, 1, 3, 5, 2, 4)
    total = chans * frames_here
    pieces = pieces.reshape(-1, COARSE, 2, stns * here, total)
    place = onehot(station_slot, jnp.arange(stns * here, dtype=jnp.int32))
    own = jnp.einsum("ar,jkprf->jkpaf", place, pieces, preferred_element_type=f32).astype(bf16)
    both = lax.all_gather(own[None], "pol", axis=0, tiled=True)
    form = "jkrf,qjksf->jrqs"

    def dot(left, right):
        return jnp.einsum(form, left, right, preferred_element_type=f32)

    own_re, own_im, re, im = own[:, :, 0], own[:, :, 1], both[:, :, :, 0], both[:, :, :, 1]
    block = jnp.stack([dot(own_re, re) + dot(own_im, im), dot(own_im, re) - dot(own_re, im)], axis=0)
    return (block * (1.0 / (total * COARSE)))[:, :, None]


def body(voltages, fir_coeffs, flags, station_slot, chan_map):
    chans, stns = lax.axis_size("chan"), lax.axis_size("stn")
    here, stations = voltages.shape[1], station_slot.shape[0]
    fits = (
        voltages.shape[2] == FL
        and chans <= TAPS
        and here % chans == 0
        and here // chans % 16 == 0
        and here == LANES
        and stations % LANES == 0
        and CH // (chans * stns) % 16 == 0
    )
    return (fast_body if fits else general_body)(voltages, fir_coeffs, flags, station_slot, chan_map)


def solution(mesh):
    in_specs = (P(("grp", "pol"), "stn", "chan"), P(), P(("grp", "pol"), "stn"), P(), P())
    out_specs = P("grp", ("chan", "stn"), "pol", None, None, None)
    return jax.shard_map(body, mesh=mesh, in_specs=in_specs, out_specs=out_specs, check_vma=False)
```

```python
import functools
import math

import jax
import jax.numpy as jnp
import numpy as np
from jax import lax
from jax.experimental import pallas as pl
from jax.experimental.pallas import tpu as pltpu
from jax.sharding import PartitionSpec as P

TAPS = 16
FL = 4096
CH = 2048
COARSE = 8
RAD = 16
PT = FL // RAD
HALF = PT // 2
LANES = 128
BATCH = 4

f32 = jnp.float32
bf16 = jnp.bfloat16


def onehot(rows, cols):
    return (rows[:, None] == cols[None, :]).astype(bf16)


@functools.cache
def tables():
    p = np.arange(PT)[None, :]
    rows = []
    for k2 in (np.arange(HALF), PT - 1 - np.arange(HALF)):
        phase = (k2[:, None] * p % PT) * (2.0 * math.pi / PT)
        rows += [np.cos(phase), -np.sin(phase)]
    table = np.concatenate(rows) * FL**-0.5
    high = table.astype(np.float32).astype(jnp.bfloat16)
    low = (table - high.astype(np.float64)).astype(np.float32).astype(jnp.bfloat16)
    phase = np.arange(1, RAD // 2 + 1)[:, None] * p * (2.0 * math.pi / FL)
    twiddle = np.concatenate([np.cos(phase), np.sin(phase)]).astype(np.float32)
    return high, low, twiddle


def real_dft16(x):
    def dft4(a0, a1, a2, a3):
        s02, d02, s13, d13 = a0 + a2, a0 - a2, a1 + a3, a1 - a3
        return s02 + s13, d02, -d13, s02 - s13

    cols = [dft4(x[b], x[4 + b], x[8 + b], x[12 + b]) for b in range(4)]
    out = [None] * 9
    r0, r1, i1, r2 = dft4(*(cols[b][0] for b in range(4)))
    out[0], out[4], out[8] = (r0, None), (r1, i1), (r2, None)
    h = math.sqrt(0.5)
    v0, v1, v2, v3 = (cols[b][3] for b in range(4))
    pr, pi = h * (v1 - v3), -h * (v1 + v3)
    out[2] = (v0 + pr, pi - v2)
    out[6] = (v0 - pr, v2 + pi)
    c1, s1 = math.cos(math.pi / 8), math.sin(math.pi / 8)
    re0, im0 = cols[0][1], cols[0][2]
    re1 = cols[1][1] * c1 + cols[1][2] * s1
    im1 = cols[1][2] * c1 - cols[1][1] * s1
    re2 = (cols[2][1] + cols[2][2]) * h
    im2 = (cols[2][2] - cols[2][1]) * h
    re3 = cols[3][1] * s1 + cols[3][2] * c1
    im3 = cols[3][2] * s1 - cols[3][1] * c1
    ar, ai, br, bi = re0 + re2, im0 + im2, re0 - re2, im0 - im2
    cr, ci, dr, di = re1 + re3, im1 + im3, re1 - re3, im1 - im3
    out[1] = (ar + cr, ai + ci)
    out[5] = (br + di, bi - dr)
    out[7] = (ar - cr, ci - ai)
    out[3] = (br - di, -bi - dr)
    return out


def split(value):
    high = value.astype(bf16)
    return high, (value - high.astype(f32)).astype(bf16)


def filterbank_kernel(frames, rows, offset, share, chan_ref, *refs):
    volts, *blocks = refs[:frames]
    fir, flag, twiddle, dft_hi, dft_lo, select = refs[frames : frames + 6]
    outs = refs[frames + 6 : -5]
    x, u_hi, u_lo, spec, sem = refs[-5:]
    total = frames * rows
    chan = chan_ref[0]
    begin = pl.multiple_of(chan * share + offset, rows)
    load = pltpu.make_async_copy(volts.at[0, pl.ds(begin, rows)], x.at[chan], sem)
    load.start()
    for d in range(1, frames):
        x[lax.rem(chan + frames - d, frames)] = blocks[d - 1][...]
    load.wait()
    step = 16
    halves = PT // LANES
    for f in range(frames):

        def unit(i, carry, f=f):
            at = pl.multiple_of(i // halves * step, step)
            base = pl.multiple_of(i % halves * LANES, LANES)
            filtered = []
            for q in range(RAD):
                lanes = pl.ds(pl.multiple_of(PT * q + base, LANES), LANES)
                acc = None
                for lag in range(f + 1):
                    tap = TAPS - 1 - lag
                    term = fir[tap : tap + 1, lanes] * x[f - lag, pl.ds(at, step), lanes].astype(f32)
                    acc = term if acc is None else acc + term
                filtered.append(acc)
            parts = []
            for c, (re, im) in enumerate(real_dft16(filtered)):
                if c == 0:
                    parts.append(re)
                    continue
                cos = twiddle[c - 1 : c, pl.ds(base, LANES)]
                sin = twiddle[RAD // 2 + c - 1 : RAD // 2 + c, pl.ds(base, LANES)]
                parts += [re * cos, -re * sin] if im is None else [re * cos + im * sin, im * cos - re * sin]
            for n, part in enumerate(parts):
                high, low = split(part)
                to = (n, pl.ds(pl.multiple_of(f * rows + at, step), step), pl.ds(base, LANES))
                u_hi[to] = high
                u_lo[to] = low
            return carry

        lax.fori_loop(0, rows // step * halves, unit, 0)
    contract = (((1,), (1,)), ((), ()))

    def three(at, count, outputs):
        a = u_hi[pl.ds(at, count)].reshape(count * total, PT)
        b = u_lo[pl.ds(at, count)].reshape(count * total, PT)
        hi, lo = dft_hi[:outputs], dft_lo[:outputs]
        out = lax.dot_general(hi, a, contract, preferred_element_type=f32)
        out = out + lax.dot_general(hi, b, contract, preferred_element_type=f32)
        return out + lax.dot_general(lo, a, contract, preferred_element_type=f32)

    lane = lax.broadcasted_iota(jnp.int32, (1, flag.shape[1]), 1)
    mine = pltpu.roll(flag[...].astype(f32), lax.rem(2 * flag.shape[1] - begin, flag.shape[1]), 1)
    keep = mine
    for f in range(1, frames):
        keep = jnp.where(lane >= f * rows, pltpu.roll(mine, f * rows, 1), keep)
    keep = keep[:, :total]

    def put(c, re, im):
        spec[c, :, :total] = (re * keep).astype(bf16)
        spec[c, :, total:] = (im * keep).astype(bf16)

    def pair(c, carry):
        got = three(2 * c - 1, 2, 2 * PT)
        re, im = got[:, :total], got[:, total:]
        put(c, re[:HALF] - im[HALF:PT], re[HALF:PT] + im[:HALF])
        o = PT + HALF
        put(RAD - c, re[PT:o] - im[o:], -(re[o:] + im[PT:o]))
        return carry

    got = three(0, 1, PT)
    put(0, got[:HALF], got[HALF:])
    got = three(RAD - 1, 2, PT)
    re, im = got[:, :total], got[:, total:]
    put(RAD // 2, re[:HALF] - im[HALF:], re[HALF:] + im[:HALF])
    lax.fori_loop(1, RAD // 2, pair, 0, unroll=True)
    right = spec[...].reshape(CH, 2 * total)
    size = CH // len(outs)
    for first in range(0, len(outs), BATCH):
        got = jnp.dot(select[first * size : (first + BATCH) * size], right, preferred_element_type=f32).astype(bf16)
        for d in range(BATCH):
            outs[first + d][...] = got[d * size : (d + 1) * size]


def filterbank(chan, volts, blocks, fir, flag, select, owners, offset, share):
    frames, rows = len(blocks) + 1, blocks[0].shape[0]
    total = frames * rows
    vmem = pl.BlockSpec(memory_space=pltpu.VMEM)
    high, low, twiddle = (jnp.asarray(t) for t in tables())
    return pl.pallas_call(
        functools.partial(filterbank_kernel, frames, rows, offset, share),
        out_shape=[jax.ShapeDtypeStruct((CH // owners, 2 * total), bf16)] * owners,
        in_specs=[pl.BlockSpec(memory_space=pltpu.SMEM), pl.BlockSpec(memory_space=pl.ANY)] + [vmem] * (frames + 5),
        out_specs=[vmem] * owners,
        scratch_shapes=[
            pltpu.VMEM((frames, rows, FL), bf16),
            pltpu.VMEM((RAD + 1, total, PT), bf16),
            pltpu.VMEM((RAD + 1, total, PT), bf16),
            pltpu.VMEM((RAD, HALF, 2 * total), bf16),
            pltpu.SemaphoreType.DMA,
        ],
        compiler_params=pltpu.CompilerParams(vmem_limit_bytes=24 << 20),
        name="filterbank",
    )(chan, volts, *blocks, fir, flag, twiddle, high, low, select)


def order_kernel(pieces, *refs):
    place, out, turned = refs[pieces:]
    half = refs[0].shape[1] // 2
    slots = refs[0].shape[0]
    parts = []
    for part in range(2):
        rows = jnp.concatenate([refs[d][:, part * half : (part + 1) * half] for d in range(pieces)], axis=1)
        got = jnp.dot(rows, place[...], preferred_element_type=f32)
        parts.append(got.reshape(slots // COARSE, 1, COARSE, got.shape[1]))
    re, im = parts
    shape = (2 * slots, re.shape[3])
    out[...] = jnp.concatenate([re, im], axis=1).reshape(shape).astype(bf16)
    turned[...] = jnp.concatenate([im, -re], axis=1).reshape(shape).astype(bf16)


def order(blocks, place):
    slots = blocks[0].shape[0]
    vmem = pl.BlockSpec(memory_space=pltpu.VMEM)
    shape = jax.ShapeDtypeStruct((2 * slots, place.shape[1]), bf16)
    return pl.pallas_call(
        functools.partial(order_kernel, len(blocks)),
        out_shape=[shape, shape],
        in_specs=[vmem] * (len(blocks) + 1),
        out_specs=[vmem] * 2,
        compiler_params=pltpu.CompilerParams(vmem_limit_bytes=16 << 20),
        name="order",
    )(*blocks, place)


def gram_kernel(frames, start, scale, pol_ref, own, turned, other, *refs):
    out, ring, sems = refs[-3:]
    stations = own.shape[1] // frames
    tiles = stations // LANES
    first = pol_ref[0] == 0
    turns = (((0,), (0,)), ((), ()))
    count = own.shape[0] // (2 * COARSE)
    depth = ring.shape[0]

    def copies(j):
        slot = lax.rem(j, depth)
        return [
            pltpu.make_async_copy(ring.at[slot, part], out.at[part, start + j], sems.at[slot, part])
            for part in range(2)
        ]

    def one(j, carry):
        slot = lax.rem(j, depth)

        @pl.when(j >= depth)
        def _():
            for copy in copies(j - depth):
                copy.wait()

        def stack(ref):
            rows = pl.ds(pl.multiple_of(2 * COARSE * j, 2 * COARSE), 2 * COARSE)
            return jnp.concatenate([ref[rows, f * stations : (f + 1) * stations] for f in range(frames)], axis=0)

        mine, mine_turned, theirs = stack(own), stack(turned), stack(other)
        right = jnp.concatenate([jnp.where(first, mine, theirs), jnp.where(first, theirs, mine)], axis=1)
        for part, left in enumerate((mine, mine_turned)):
            got = lax.dot_general(left, right, turns, preferred_element_type=f32) * scale
            for q in range(2):
                for t in range(tiles):
                    at = q * stations + t * LANES
                    ring[slot, part, pl.ds(2 * t + q, stations, stride=2 * tiles), :] = got[:, at : at + LANES]
        for copy in copies(j):
            copy.start()
        return carry

    lax.fori_loop(0, count, one, 0)
    for j in range(count - depth, count):
        for copy in copies(j):
            copy.wait()


def gram(pol, own, turned, other, frames, coarse, start, into):
    count = own.shape[0] // (2 * COARSE)
    stations = own.shape[1] // frames
    rows = stations * 2 * (stations // LANES)
    depth = min(4, count)
    vmem, hbm = pl.BlockSpec(memory_space=pltpu.VMEM), pl.BlockSpec(memory_space=pltpu.HBM)
    more = [] if into is None else [into]
    return pl.pallas_call(
        functools.partial(gram_kernel, frames, start, 1.0 / (frames * COARSE)),
        out_shape=jax.ShapeDtypeStruct((2, coarse, rows, LANES), f32),
        in_specs=[pl.BlockSpec(memory_space=pltpu.SMEM), vmem, vmem, vmem] + [hbm] * len(more),
        out_specs=hbm,
        scratch_shapes=[pltpu.VMEM((depth, 2, rows, LANES), f32), pltpu.SemaphoreType.DMA((depth, 2))],
        input_output_aliases={4: 0} if more else {},
        compiler_params=pltpu.CompilerParams(vmem_limit_bytes=16 << 20),
        name="gram",
    )(pol, own, turned, other, *more)


def rolled(array, axis, start, size):
    return lax.dynamic_slice_in_dim(jnp.concatenate([array, array], axis=axis), start, size, axis=axis)


def groups_of(rows):
    return [(0, rows)]


def fast_body(voltages, fir_coeffs, flags, station_slot, chan_map):
    chans, stns = lax.axis_size("chan"), lax.axis_size("stn")
    chan, stn, pol = lax.axis_index("chan"), lax.axis_index("stn"), lax.axis_index("pol")
    here = voltages.shape[1]
    stations = station_slot.shape[0]
    frames = chans
    rows = here // chans
    owners = chans * stns
    slots = CH // owners
    coarse = slots // COARSE
    groups = groups_of(rows)
    shares = voltages.reshape(chans, rows, FL)
    blocks = []
    for offset, size in groups:
        blocks.append([])
        for d in range(1, chans):
            share = lax.dynamic_index_in_dim(shares[:, offset : offset + size], (chan + d) % chans, 0, keepdims=False)
            blocks[-1].append(lax.ppermute(share, "chan", [(i, (i + d) % chans) for i in range(chans)]))
    lane_of = (chan_map % RAD) * HALF + chan_map // RAD
    lane_of = rolled(rolled(lane_of.reshape(chans, stns, slots), 0, chan, chans), 1, stn, stns)
    select = onehot(lane_of.reshape(CH), jnp.arange(CH, dtype=jnp.int32))
    got = []
    place = []
    dist = jnp.arange(owners, dtype=jnp.int32)
    row0 = (stn - dist % stns) % stns * here + (chan - dist // stns) % chans * rows
    col = station_slot[None, :] + stations * jnp.arange(frames, dtype=jnp.int32)[:, None]
    for (offset, size), block in zip(groups, blocks, strict=True):
        pieces = filterbank(
            chan.reshape(1), voltages, block, fir_coeffs, flags, select, owners, offset, rows
        )
        got.append(pieces[0])
        for d in range(1, owners):
            dc, ds = divmod(d, stns)
            route = [
                (i * stns + j, (i + dc) % chans * stns + (j + ds) % stns) for i in range(chans) for j in range(stns)
            ]
            got.append(lax.ppermute(pieces[d], ("chan", "stn"), route))
        row = row0[:, None, None] + offset + jnp.arange(size, dtype=jnp.int32)[None, None, :]
        row = row + stations * jnp.arange(frames, dtype=jnp.int32)[None, :, None]
        place.append(row.reshape(-1))
    place = onehot(jnp.concatenate(place), col.reshape(-1))
    own, turned = order(got, place)
    other = lax.ppermute(own, "pol", [(0, 1), (1, 0)])
    out = gram(pol.reshape(1), own, turned, other, frames, coarse, 0, None)
    tiles = stations // LANES
    out = out.reshape(2, -1, stations, tiles, 2, LANES).transpose(0, 1, 2, 4, 3, 5)
    return out.reshape(2, -1, 1, stations, 2, stations)


def general_body(voltages, fir_coeffs, flags, station_slot, chan_map):
    high = lax.Precision.HIGHEST
    here = voltages.shape[1]
    chans, stns = lax.axis_size("chan"), lax.axis_size("stn")
    frames_here = voltages.shape[2] // FL
    frames = voltages.reshape(here, frames_here, FL)
    history = []
    for distance in range(1, (TAPS - 1 + frames_here - 1) // frames_here + 1):
        route = [(i - distance, i) for i in range(distance, chans)]
        history = [lax.ppermute(frames, "chan", route)] + history
    window = jnp.concatenate(history + [frames], axis=1)
    window = window[:, window.shape[1] - frames_here - TAPS + 1 :]
    filtered = jnp.zeros((here, frames_here, FL), f32)
    for tap in range(TAPS):
        filtered = filtered + fir_coeffs[tap][None, None, :] * window[:, tap : tap + frames_here, :].astype(f32)
    side = math.isqrt(FL)

    def angles(rows, cols, period):
        product = jnp.arange(rows, dtype=jnp.int32)[:, None] * jnp.arange(cols, dtype=jnp.int32)[None, :]
        phase = (product % period).astype(f32) * (2.0 * math.pi / period)
        return jnp.cos(phase), jnp.sin(phase)

    grid = filtered.reshape(here, frames_here, side, side)
    cos, sin = angles(side, side, side)
    re = jnp.einsum("sfqp,qc->sfpc", grid, cos, precision=high)
    im = -jnp.einsum("sfqp,qc->sfpc", grid, sin, precision=high)
    cos, sin = angles(side, side, FL)
    re, im = re * cos + im * sin, im * cos - re * sin
    cos, sin = angles(side, side // 2, side)
    form = "sfpc,pk->kcfs"
    out_re = jnp.einsum(form, re, cos, precision=high) + jnp.einsum(form, im, sin, precision=high)
    out_im = jnp.einsum(form, im, cos, precision=high) - jnp.einsum(form, re, sin, precision=high)
    weight = jnp.tile(flags[0].astype(f32), frames_here) * FL**-0.5
    shape = (CH, 1, frames_here * here)
    spectra = jnp.concatenate(
        [(out_re.reshape(shape) * weight).astype(bf16), (out_im.reshape(shape) * weight).astype(bf16)], axis=1
    )
    select = onehot(chan_map, jnp.arange(CH, dtype=jnp.int32))
    spectra = jnp.einsum("sc,cpn->spn", select, spectra, preferred_element_type=f32).astype(bf16)
    pieces = lax.all_to_all(spectra, ("chan", "stn"), split_axis=0, concat_axis=2, tiled=True)
    pieces = pieces.reshape(-1, 2, chans, stns, frames_here, here).transpose(0, 1, 3, 5, 2, 4)
    total = chans * frames_here
    pieces = pieces.reshape(-1, COARSE, 2, stns * here, total)
    place = onehot(station_slot, jnp.arange(stns * here, dtype=jnp.int32))
    own = jnp.einsum("ar,jkprf->jkpaf", place, pieces, preferred_element_type=f32).astype(bf16)
    both = lax.all_gather(own[None], "pol", axis=0, tiled=True)
    form = "jkrf,qjksf->jrqs"

    def dot(left, right):
        return jnp.einsum(form, left, right, preferred_element_type=f32)

    own_re, own_im, re, im = own[:, :, 0], own[:, :, 1], both[:, :, :, 0], both[:, :, :, 1]
    block = jnp.stack([dot(own_re, re) + dot(own_im, im), dot(own_im, re) - dot(own_re, im)], axis=0)
    return (block * (1.0 / (total * COARSE)))[:, :, None]


def body(voltages, fir_coeffs, flags, station_slot, chan_map):
    chans, stns = lax.axis_size("chan"), lax.axis_size("stn")
    here, stations = voltages.shape[1], station_slot.shape[0]
    fits = (
        voltages.shape[2] == FL
        and chans <= TAPS
        and here % chans == 0
        and here // chans % 16 == 0
        and here == LANES
        and stations % LANES == 0
        and CH // (chans * stns) % 16 == 0
    )
    return (fast_body if fits else general_body)(voltages, fir_coeffs, flags, station_slot, chan_map)


def solution(mesh):
    in_specs = (P(("grp", "pol"), "stn", "chan"), P(), P(("grp", "pol"), "stn"), P(), P())
    out_specs = P("grp", ("chan", "stn"), "pol", None, None, None)
    return jax.shard_map(body, mesh=mesh, in_specs=in_specs, out_specs=out_specs, check_vma=False)
```

```python
import functools
import math

import jax
import jax.numpy as jnp
import numpy as np
from jax import lax
from jax.experimental import pallas as pl
from jax.experimental.pallas import tpu as pltpu
from jax.sharding import PartitionSpec as P

TAPS = 16
FL = 4096
CH = 2048
COARSE = 8
RAD = 16
PT = FL // RAD
HALF = PT // 2
LANES = 128
BATCH = 4

f32 = jnp.float32
bf16 = jnp.bfloat16


def onehot(rows, cols):
    return (rows[:, None] == cols[None, :]).astype(bf16)


@functools.cache
def tables():
    p = np.arange(PT)[None, :]
    rows = []
    for k2 in (np.arange(HALF), PT - 1 - np.arange(HALF)):
        phase = (k2[:, None] * p % PT) * (2.0 * math.pi / PT)
        rows += [np.cos(phase), -np.sin(phase)]
    table = np.concatenate(rows) * FL**-0.5
    high = table.astype(np.float32).astype(jnp.bfloat16)
    low = (table - high.astype(np.float64)).astype(np.float32).astype(jnp.bfloat16)
    phase = np.arange(1, RAD // 2 + 1)[:, None] * p * (2.0 * math.pi / FL)
    twiddle = np.concatenate([np.cos(phase), np.sin(phase)]).astype(np.float32)
    return high, low, twiddle


def real_dft16(x):
    def dft4(a0, a1, a2, a3):
        s02, d02, s13, d13 = a0 + a2, a0 - a2, a1 + a3, a1 - a3
        return s02 + s13, d02, -d13, s02 - s13

    cols = [dft4(x[b], x[4 + b], x[8 + b], x[12 + b]) for b in range(4)]
    out = [None] * 9
    r0, r1, i1, r2 = dft4(*(cols[b][0] for b in range(4)))
    out[0], out[4], out[8] = (r0, None), (r1, i1), (r2, None)
    h = math.sqrt(0.5)
    v0, v1, v2, v3 = (cols[b][3] for b in range(4))
    pr, pi = h * (v1 - v3), -h * (v1 + v3)
    out[2] = (v0 + pr, pi - v2)
    out[6] = (v0 - pr, v2 + pi)
    c1, s1 = math.cos(math.pi / 8), math.sin(math.pi / 8)
    re0, im0 = cols[0][1], cols[0][2]
    re1 = cols[1][1] * c1 + cols[1][2] * s1
    im1 = cols[1][2] * c1 - cols[1][1] * s1
    re2 = (cols[2][1] + cols[2][2]) * h
    im2 = (cols[2][2] - cols[2][1]) * h
    re3 = cols[3][1] * s1 + cols[3][2] * c1
    im3 = cols[3][2] * s1 - cols[3][1] * c1
    ar, ai, br, bi = re0 + re2, im0 + im2, re0 - re2, im0 - im2
    cr, ci, dr, di = re1 + re3, im1 + im3, re1 - re3, im1 - im3
    out[1] = (ar + cr, ai + ci)
    out[5] = (br + di, bi - dr)
    out[7] = (ar - cr, ci - ai)
    out[3] = (br - di, -bi - dr)
    return out


def split(value):
    high = value.astype(bf16)
    return high, (value - high.astype(f32)).astype(bf16)


def filterbank_kernel(frames, rows, offset, share, chan_ref, *refs):
    volts, *blocks = refs[:frames]
    blocks = blocks[::-1]
    fir, flag, twiddle, dft_hi, dft_lo, select = refs[frames : frames + 6]
    outs = refs[frames + 6 : -5]
    x, u_hi, u_lo, spec, sem = refs[-5:]
    total = frames * rows
    chan = chan_ref[0]
    begin = pl.multiple_of(chan * share + offset, rows)
    load = pltpu.make_async_copy(volts.at[0, pl.ds(begin, rows)], x.at[chan], sem)
    load.start()
    for d in range(1, frames):
        x[jnp.bitwise_xor(chan, d)] = blocks[d - 1][...]
    load.wait()
    step = 16
    halves = PT // LANES
    for f in range(frames):

        def unit(i, carry, f=f):
            at = pl.multiple_of(i // halves * step, step)
            base = pl.multiple_of(i % halves * LANES, LANES)
            filtered = []
            for q in range(RAD):
                lanes = pl.ds(pl.multiple_of(PT * q + base, LANES), LANES)
                acc = None
                for lag in range(f + 1):
                    tap = TAPS - 1 - lag
                    term = fir[tap : tap + 1, lanes] * x[f - lag, pl.ds(at, step), lanes].astype(f32)
                    acc = term if acc is None else acc + term
                filtered.append(acc)
            parts = []
            for c, (re, im) in enumerate(real_dft16(filtered)):
                if c == 0:
                    parts.append(re)
                    continue
                cos = twiddle[c - 1 : c, pl.ds(base, LANES)]
                sin = twiddle[RAD // 2 + c - 1 : RAD // 2 + c, pl.ds(base, LANES)]
                parts += [re * cos, -re * sin] if im is None else [re * cos + im * sin, im * cos - re * sin]
            for n, part in enumerate(parts):
                high, low = split(part)
                to = (n, pl.ds(pl.multiple_of(f * rows + at, step), step), pl.ds(base, LANES))
                u_hi[to] = high
                u_lo[to] = low
            return carry

        lax.fori_loop(0, rows // step * halves, unit, 0)
    contract = (((1,), (1,)), ((), ()))

    def three(at, count, outputs):
        a = u_hi[pl.ds(at, count)].reshape(count * total, PT)
        b = u_lo[pl.ds(at, count)].reshape(count * total, PT)
        hi, lo = dft_hi[:outputs], dft_lo[:outputs]
        out = lax.dot_general(hi, a, contract, preferred_element_type=f32)
        out = out + lax.dot_general(hi, b, contract, preferred_element_type=f32)
        return out + lax.dot_general(lo, a, contract, preferred_element_type=f32)

    lane = lax.broadcasted_iota(jnp.int32, (1, flag.shape[1]), 1)
    mine = pltpu.roll(flag[...].astype(f32), lax.rem(2 * flag.shape[1] - begin, flag.shape[1]), 1)
    keep = mine
    for f in range(1, frames):
        keep = jnp.where(lane >= f * rows, pltpu.roll(mine, f * rows, 1), keep)
    keep = keep[:, :total]

    def put(c, re, im):
        spec[c, :, :total] = (re * keep).astype(bf16)
        spec[c, :, total:] = (im * keep).astype(bf16)

    def pair(c, carry):
        got = three(2 * c - 1, 2, 2 * PT)
        re, im = got[:, :total], got[:, total:]
        put(c, re[:HALF] - im[HALF:PT], re[HALF:PT] + im[:HALF])
        o = PT + HALF
        put(RAD - c, re[PT:o] - im[o:], -(re[o:] + im[PT:o]))
        return carry

    got = three(0, 1, PT)
    put(0, got[:HALF], got[HALF:])
    got = three(RAD - 1, 2, PT)
    re, im = got[:, :total], got[:, total:]
    put(RAD // 2, re[:HALF] - im[HALF:], re[HALF:] + im[:HALF])
    lax.fori_loop(1, RAD // 2, pair, 0, unroll=True)
    right = spec[...].reshape(CH, 2 * total)
    size = CH // len(outs)
    for first in range(0, len(outs), BATCH):
        got = jnp.dot(select[first * size : (first + BATCH) * size], right, preferred_element_type=f32).astype(bf16)
        for d in range(BATCH):
            outs[first + d][...] = got[d * size : (d + 1) * size]


def filterbank(chan, volts, blocks, fir, flag, select, owners, offset, share):
    frames, rows = len(blocks) + 1, blocks[0].shape[0]
    total = frames * rows
    vmem = pl.BlockSpec(memory_space=pltpu.VMEM)
    high, low, twiddle = (jnp.asarray(t) for t in tables())
    return pl.pallas_call(
        functools.partial(filterbank_kernel, frames, rows, offset, share),
        out_shape=[jax.ShapeDtypeStruct((CH // owners, 2 * total), bf16)] * owners,
        in_specs=[pl.BlockSpec(memory_space=pltpu.SMEM), pl.BlockSpec(memory_space=pl.ANY)] + [vmem] * (frames + 5),
        out_specs=[vmem] * owners,
        scratch_shapes=[
            pltpu.VMEM((frames, rows, FL), bf16),
            pltpu.VMEM((RAD + 1, total, PT), bf16),
            pltpu.VMEM((RAD + 1, total, PT), bf16),
            pltpu.VMEM((RAD, HALF, 2 * total), bf16),
            pltpu.SemaphoreType.DMA,
        ],
        compiler_params=pltpu.CompilerParams(vmem_limit_bytes=24 << 20),
        name="filterbank",
    )(chan, volts, *blocks[::-1], fir, flag, twiddle, high, low, select)


def order_kernel(pieces, *refs):
    place, out, turned = refs[pieces:]
    half = refs[0].shape[1] // 2
    slots = refs[0].shape[0]
    parts = []
    for part in range(2):
        rows = jnp.concatenate([refs[d][:, part * half : (part + 1) * half] for d in range(pieces)], axis=1)
        got = jnp.dot(rows, place[...], preferred_element_type=f32)
        parts.append(got.reshape(slots // COARSE, 1, COARSE, got.shape[1]))
    re, im = parts
    shape = (2 * slots, re.shape[3])
    out[...] = jnp.concatenate([re, im], axis=1).reshape(shape).astype(bf16)
    turned[...] = jnp.concatenate([im, -re], axis=1).reshape(shape).astype(bf16)


def order(blocks, place):
    slots = blocks[0].shape[0]
    vmem = pl.BlockSpec(memory_space=pltpu.VMEM)
    shape = jax.ShapeDtypeStruct((2 * slots, place.shape[1]), bf16)
    return pl.pallas_call(
        functools.partial(order_kernel, len(blocks)),
        out_shape=[shape, shape],
        in_specs=[vmem] * (len(blocks) + 1),
        out_specs=[vmem] * 2,
        compiler_params=pltpu.CompilerParams(vmem_limit_bytes=16 << 20),
        name="order",
    )(*blocks, place)


def gram_kernel(frames, start, scale, pol_ref, own, turned, other, *refs):
    out, ring, sems = refs[-3:]
    stations = own.shape[1] // frames
    tiles = stations // LANES
    first = pol_ref[0] == 0
    turns = (((0,), (0,)), ((), ()))
    count = own.shape[0] // (2 * COARSE)
    depth = ring.shape[0]

    def copies(j):
        slot = lax.rem(j, depth)
        return [
            pltpu.make_async_copy(ring.at[slot, part], out.at[part, start + j], sems.at[slot, part])
            for part in range(2)
        ]

    def one(j, carry):
        slot = lax.rem(j, depth)

        @pl.when(j >= depth)
        def _():
            for copy in copies(j - depth):
                copy.wait()

        def stack(ref):
            rows = pl.ds(pl.multiple_of(2 * COARSE * j, 2 * COARSE), 2 * COARSE)
            return jnp.concatenate([ref[rows, f * stations : (f + 1) * stations] for f in range(frames)], axis=0)

        mine, mine_turned, theirs = stack(own), stack(turned), stack(other)
        right = jnp.concatenate([jnp.where(first, mine, theirs), jnp.where(first, theirs, mine)], axis=1)
        for part, left in enumerate((mine, mine_turned)):
            got = lax.dot_general(left, right, turns, preferred_element_type=f32) * scale
            for q in range(2):
                for t in range(tiles):
                    at = q * stations + t * LANES
                    ring[slot, part, pl.ds(2 * t + q, stations, stride=2 * tiles), :] = got[:, at : at + LANES]
        for copy in copies(j):
            copy.start()
        return carry

    lax.fori_loop(0, count, one, 0)
    for j in range(count - depth, count):
        for copy in copies(j):
            copy.wait()


def gram(pol, own, turned, other, frames, coarse, start, into):
    count = own.shape[0] // (2 * COARSE)
    stations = own.shape[1] // frames
    rows = stations * 2 * (stations // LANES)
    depth = min(4, count)
    vmem, hbm = pl.BlockSpec(memory_space=pltpu.VMEM), pl.BlockSpec(memory_space=pltpu.HBM)
    more = [] if into is None else [into]
    return pl.pallas_call(
        functools.partial(gram_kernel, frames, start, 1.0 / (frames * COARSE)),
        out_shape=jax.ShapeDtypeStruct((2, coarse, rows, LANES), f32),
        in_specs=[pl.BlockSpec(memory_space=pltpu.SMEM), vmem, vmem, vmem] + [hbm] * len(more),
        out_specs=hbm,
        scratch_shapes=[pltpu.VMEM((depth, 2, rows, LANES), f32), pltpu.SemaphoreType.DMA((depth, 2))],
        input_output_aliases={4: 0} if more else {},
        compiler_params=pltpu.CompilerParams(vmem_limit_bytes=16 << 20),
        name="gram",
    )(pol, own, turned, other, *more)


def rolled(array, axis, start, size):
    return lax.dynamic_slice_in_dim(jnp.concatenate([array, array], axis=axis), start, size, axis=axis)


def groups_of(rows):
    return [(0, rows)]


def fast_body(voltages, fir_coeffs, flags, station_slot, chan_map):
    chans, stns = lax.axis_size("chan"), lax.axis_size("stn")
    chan, stn, pol = lax.axis_index("chan"), lax.axis_index("stn"), lax.axis_index("pol")
    here = voltages.shape[1]
    stations = station_slot.shape[0]
    frames = chans
    rows = here // chans
    owners = chans * stns
    slots = CH // owners
    coarse = slots // COARSE
    groups = groups_of(rows)
    shares = voltages.reshape(chans, rows, FL)
    blocks = []
    for offset, size in groups:
        blocks.append([])
        for d in range(1, chans):
            share = lax.dynamic_index_in_dim(shares[:, offset : offset + size], chan ^ d, 0, keepdims=False)
            blocks[-1].append(lax.ppermute(share, "chan", [(i, i ^ d) for i in range(chans)]))
    lane_of = (chan_map % RAD) * HALF + chan_map // RAD
    lane_of = rolled(rolled(lane_of.reshape(chans, stns, slots), 0, chan, chans), 1, stn, stns)
    select = onehot(lane_of.reshape(CH), jnp.arange(CH, dtype=jnp.int32))
    got = []
    place = []
    dist = jnp.arange(owners, dtype=jnp.int32)
    row0 = (stn - dist % stns) % stns * here + (chan - dist // stns) % chans * rows
    col = station_slot[None, :] + stations * jnp.arange(frames, dtype=jnp.int32)[:, None]
    for (offset, size), block in zip(groups, blocks, strict=True):
        pieces = filterbank(
            chan.reshape(1), voltages, block, fir_coeffs, flags, select, owners, offset, rows
        )
        got.append(pieces[0])
        for d in range(1, owners):
            dc, ds = divmod(d, stns)
            route = [
                (i * stns + j, (i + dc) % chans * stns + (j + ds) % stns) for i in range(chans) for j in range(stns)
            ]
            got.append(lax.ppermute(pieces[d], ("chan", "stn"), route))
        row = row0[:, None, None] + offset + jnp.arange(size, dtype=jnp.int32)[None, None, :]
        row = row + stations * jnp.arange(frames, dtype=jnp.int32)[None, :, None]
        place.append(row.reshape(-1))
    place = onehot(jnp.concatenate(place), col.reshape(-1))
    own, turned = order(got, place)
    other = lax.ppermute(own, "pol", [(0, 1), (1, 0)])
    out = gram(pol.reshape(1), own, turned, other, frames, coarse, 0, None)
    tiles = stations // LANES
    out = out.reshape(2, -1, stations, tiles, 2, LANES).transpose(0, 1, 2, 4, 3, 5)
    return out.reshape(2, -1, 1, stations, 2, stations)


def general_body(voltages, fir_coeffs, flags, station_slot, chan_map):
    high = lax.Precision.HIGHEST
    here = voltages.shape[1]
    chans, stns = lax.axis_size("chan"), lax.axis_size("stn")
    frames_here = voltages.shape[2] // FL
    frames = voltages.reshape(here, frames_here, FL)
    history = []
    for distance in range(1, (TAPS - 1 + frames_here - 1) // frames_here + 1):
        route = [(i - distance, i) for i in range(distance, chans)]
        history = [lax.ppermute(frames, "chan", route)] + history
    window = jnp.concatenate(history + [frames], axis=1)
    window = window[:, window.shape[1] - frames_here - TAPS + 1 :]
    filtered = jnp.zeros((here, frames_here, FL), f32)
    for tap in range(TAPS):
        filtered = filtered + fir_coeffs[tap][None, None, :] * window[:, tap : tap + frames_here, :].astype(f32)
    side = math.isqrt(FL)

    def angles(rows, cols, period):
        product = jnp.arange(rows, dtype=jnp.int32)[:, None] * jnp.arange(cols, dtype=jnp.int32)[None, :]
        phase = (product % period).astype(f32) * (2.0 * math.pi / period)
        return jnp.cos(phase), jnp.sin(phase)

    grid = filtered.reshape(here, frames_here, side, side)
    cos, sin = angles(side, side, side)
    re = jnp.einsum("sfqp,qc->sfpc", grid, cos, precision=high)
    im = -jnp.einsum("sfqp,qc->sfpc", grid, sin, precision=high)
    cos, sin = angles(side, side, FL)
    re, im = re * cos + im * sin, im * cos - re * sin
    cos, sin = angles(side, side // 2, side)
    form = "sfpc,pk->kcfs"
    out_re = jnp.einsum(form, re, cos, precision=high) + jnp.einsum(form, im, sin, precision=high)
    out_im = jnp.einsum(form, im, cos, precision=high) - jnp.einsum(form, re, sin, precision=high)
    weight = jnp.tile(flags[0].astype(f32), frames_here) * FL**-0.5
    shape = (CH, 1, frames_here * here)
    spectra = jnp.concatenate(
        [(out_re.reshape(shape) * weight).astype(bf16), (out_im.reshape(shape) * weight).astype(bf16)], axis=1
    )
    select = onehot(chan_map, jnp.arange(CH, dtype=jnp.int32))
    spectra = jnp.einsum("sc,cpn->spn", select, spectra, preferred_element_type=f32).astype(bf16)
    pieces = lax.all_to_all(spectra, ("chan", "stn"), split_axis=0, concat_axis=2, tiled=True)
    pieces = pieces.reshape(-1, 2, chans, stns, frames_here, here).transpose(0, 1, 3, 5, 2, 4)
    total = chans * frames_here
    pieces = pieces.reshape(-1, COARSE, 2, stns * here, total)
    place = onehot(station_slot, jnp.arange(stns * here, dtype=jnp.int32))
    own = jnp.einsum("ar,jkprf->jkpaf", place, pieces, preferred_element_type=f32).astype(bf16)
    both = lax.all_gather(own[None], "pol", axis=0, tiled=True)
    form = "jkrf,qjksf->jrqs"

    def dot(left, right):
        return jnp.einsum(form, left, right, preferred_element_type=f32)

    own_re, own_im, re, im = own[:, :, 0], own[:, :, 1], both[:, :, :, 0], both[:, :, :, 1]
    block = jnp.stack([dot(own_re, re) + dot(own_im, im), dot(own_im, re) - dot(own_re, im)], axis=0)
    return (block * (1.0 / (total * COARSE)))[:, :, None]


def body(voltages, fir_coeffs, flags, station_slot, chan_map):
    chans, stns = lax.axis_size("chan"), lax.axis_size("stn")
    here, stations = voltages.shape[1], station_slot.shape[0]
    fits = (
        voltages.shape[2] == FL
        and chans <= TAPS
        and chans & (chans - 1) == 0
        and here % chans == 0
        and here // chans % 16 == 0
        and here == LANES
        and stations % LANES == 0
        and CH // (chans * stns) % 16 == 0
    )
    return (fast_body if fits else general_body)(voltages, fir_coeffs, flags, station_slot, chan_map)


def solution(mesh):
    in_specs = (P(("grp", "pol"), "stn", "chan"), P(), P(("grp", "pol"), "stn"), P(), P())
    out_specs = P("grp", ("chan", "stn"), "pol", None, None, None)
    return jax.shard_map(body, mesh=mesh, in_specs=in_specs, out_specs=out_specs, check_vma=False)
```

```python
import functools
import math

import jax
import jax.numpy as jnp
import numpy as np
from jax import lax
from jax.experimental import pallas as pl
from jax.experimental.pallas import tpu as pltpu
from jax.sharding import PartitionSpec as P

TAPS = 16
FL = 4096
CH = 2048
COARSE = 8
RAD = 16
PT = FL // RAD
HALF = PT // 2
LANES = 128
BATCH = 4

f32 = jnp.float32
bf16 = jnp.bfloat16


def onehot(rows, cols):
    return (rows[:, None] == cols[None, :]).astype(bf16)


@functools.cache
def tables():
    p = np.arange(PT)[None, :]
    rows = []
    for k2 in (np.arange(HALF), PT - 1 - np.arange(HALF)):
        phase = (k2[:, None] * p % PT) * (2.0 * math.pi / PT)
        rows += [np.cos(phase), -np.sin(phase)]
    table = np.concatenate(rows) * FL**-0.5
    high = table.astype(np.float32).astype(jnp.bfloat16)
    low = (table - high.astype(np.float64)).astype(np.float32).astype(jnp.bfloat16)
    phase = np.arange(1, RAD // 2 + 1)[:, None] * p * (2.0 * math.pi / FL)
    twiddle = np.concatenate([np.cos(phase), np.sin(phase)]).astype(np.float32)
    return high, low, twiddle


def real_dft16(x):
    def dft4(a0, a1, a2, a3):
        s02, d02, s13, d13 = a0 + a2, a0 - a2, a1 + a3, a1 - a3
        return s02 + s13, d02, -d13, s02 - s13

    cols = [dft4(x[b], x[4 + b], x[8 + b], x[12 + b]) for b in range(4)]
    out = [None] * 9
    r0, r1, i1, r2 = dft4(*(cols[b][0] for b in range(4)))
    out[0], out[4], out[8] = (r0, None), (r1, i1), (r2, None)
    h = math.sqrt(0.5)
    v0, v1, v2, v3 = (cols[b][3] for b in range(4))
    pr, pi = h * (v1 - v3), -h * (v1 + v3)
    out[2] = (v0 + pr, pi - v2)
    out[6] = (v0 - pr, v2 + pi)
    c1, s1 = math.cos(math.pi / 8), math.sin(math.pi / 8)
    re0, im0 = cols[0][1], cols[0][2]
    re1 = cols[1][1] * c1 + cols[1][2] * s1
    im1 = cols[1][2] * c1 - cols[1][1] * s1
    re2 = (cols[2][1] + cols[2][2]) * h
    im2 = (cols[2][2] - cols[2][1]) * h
    re3 = cols[3][1] * s1 + cols[3][2] * c1
    im3 = cols[3][2] * s1 - cols[3][1] * c1
    ar, ai, br, bi = re0 + re2, im0 + im2, re0 - re2, im0 - im2
    cr, ci, dr, di = re1 + re3, im1 + im3, re1 - re3, im1 - im3
    out[1] = (ar + cr, ai + ci)
    out[5] = (br + di, bi - dr)
    out[7] = (ar - cr, ci - ai)
    out[3] = (br - di, -bi - dr)
    return out


def split(value):
    high = value.astype(bf16)
    return high, (value - high.astype(f32)).astype(bf16)


def filterbank_kernel(frames, share, group, pieces, before, chan_ref, *refs):
    offset, rows = group
    volts, *blocks = refs[:frames]
    blocks = blocks[::-1]
    fir, flag, twiddle, dft_hi, dft_lo, *rest = refs[frames:-4]
    x, u_hi, u_lo, sem = refs[-4:]
    if pieces:
        spec = rest.pop()
    prior = [rest.pop(0) for _ in range(before)]
    select, *outs = rest
    if not pieces:
        [spec] = outs
    total = frames * rows
    whole = frames * share
    chan = chan_ref[0]
    begin = pl.multiple_of(chan * share + offset, rows)
    load = pltpu.make_async_copy(volts.at[0, pl.ds(begin, rows)], x.at[chan], sem)
    load.start()
    for d in range(1, frames):
        x[jnp.bitwise_xor(chan, d)] = blocks[d - 1][...]
    for earlier in prior:
        spec[...] = earlier[...]
    load.wait()
    step = 16
    halves = PT // LANES
    for f in range(frames):

        def unit(i, carry, f=f):
            at = pl.multiple_of(i // halves * step, step)
            base = pl.multiple_of(i % halves * LANES, LANES)
            filtered = []
            for q in range(RAD):
                lanes = pl.ds(pl.multiple_of(PT * q + base, LANES), LANES)
                acc = None
                for lag in range(f + 1):
                    tap = TAPS - 1 - lag
                    term = fir[tap : tap + 1, lanes] * x[f - lag, pl.ds(at, step), lanes].astype(f32)
                    acc = term if acc is None else acc + term
                filtered.append(acc)
            parts = []
            for c, (re, im) in enumerate(real_dft16(filtered)):
                if c == 0:
                    parts.append(re)
                    continue
                cos = twiddle[c - 1 : c, pl.ds(base, LANES)]
                sin = twiddle[RAD // 2 + c - 1 : RAD // 2 + c, pl.ds(base, LANES)]
                parts += [re * cos, -re * sin] if im is None else [re * cos + im * sin, im * cos - re * sin]
            for n, part in enumerate(parts):
                high, low = split(part)
                to = (n, pl.ds(pl.multiple_of(f * rows + at, step), step), pl.ds(base, LANES))
                u_hi[to] = high
                u_lo[to] = low
            return carry

        lax.fori_loop(0, rows // step * halves, unit, 0)
    contract = (((1,), (1,)), ((), ()))

    def three(at, count, outputs):
        a = u_hi[pl.ds(at, count)].reshape(count * total, PT)
        b = u_lo[pl.ds(at, count)].reshape(count * total, PT)
        hi, lo = dft_hi[:outputs], dft_lo[:outputs]
        out = lax.dot_general(hi, a, contract, preferred_element_type=f32)
        out = out + lax.dot_general(hi, b, contract, preferred_element_type=f32)
        return out + lax.dot_general(lo, a, contract, preferred_element_type=f32)

    lane = lax.broadcasted_iota(jnp.int32, (1, flag.shape[1]), 1)
    mine = pltpu.roll(flag[...].astype(f32), lax.rem(2 * flag.shape[1] - begin, flag.shape[1]), 1)
    keep = mine
    for f in range(1, frames):
        keep = jnp.where(lane >= f * rows, pltpu.roll(mine, f * rows, 1), keep)
    keep = keep[:, :total]
    lanes_of = [slice(part * whole + frames * offset, part * whole + frames * offset + total) for part in range(2)]

    def put(c, re, im):
        spec[c, :, lanes_of[0]] = (re * keep).astype(bf16)
        spec[c, :, lanes_of[1]] = (im * keep).astype(bf16)

    got = three(0, 1, PT)
    put(0, got[:HALF], got[HALF:])
    per = max(1, LANES // total)
    o = PT + HALF
    for first in range(1, RAD // 2 + 1, per):
        got = three(2 * first - 1, 2 * per, PT if first == RAD // 2 else 2 * PT)
        for k in range(per):
            c = first + k
            re, im = got[:, 2 * k * total : (2 * k + 1) * total], got[:, (2 * k + 1) * total : (2 * k + 2) * total]
            put(c, re[:HALF] - im[HALF:PT], re[HALF:PT] + im[:HALF])
            if c < RAD // 2:
                put(RAD - c, re[PT:o] - im[o:], -(re[o:] + im[PT:o]))
    if not pieces:
        return
    right = spec[...].reshape(CH, 2 * whole)
    size = CH // pieces
    for first in range(0, pieces, BATCH):
        got = jnp.dot(select[first * size : (first + BATCH) * size], right, preferred_element_type=f32).astype(bf16)
        for d in range(BATCH):
            outs[first + d][...] = got[d * size : (d + 1) * size]


def filterbank(chan, volts, blocks, fir, flag, share, group, prior, select, pieces):
    frames, rows = len(blocks) + 1, group[1]
    total, whole = frames * rows, frames * share
    vmem = pl.BlockSpec(memory_space=pltpu.VMEM)
    high, low, twiddle = (jnp.asarray(t) for t in tables())
    spec = (RAD, HALF, 2 * whole)
    args = [*blocks[::-1], fir, flag, twiddle, high, low] + prior + [select]
    outs = [jax.ShapeDtypeStruct((CH // pieces, 2 * whole), bf16)] * pieces if pieces else jax.ShapeDtypeStruct(spec, bf16)
    return pl.pallas_call(
        functools.partial(filterbank_kernel, frames, share, group, pieces, len(prior)),
        out_shape=outs,
        in_specs=[pl.BlockSpec(memory_space=pltpu.SMEM), pl.BlockSpec(memory_space=pl.ANY)] + [vmem] * len(args),
        out_specs=[vmem] * pieces if pieces else vmem,
        scratch_shapes=([pltpu.VMEM(spec, bf16)] if pieces else [])
        + [
            pltpu.VMEM((frames, rows, FL), bf16),
            pltpu.VMEM((RAD + 1, total, PT), bf16),
            pltpu.VMEM((RAD + 1, total, PT), bf16),
            pltpu.SemaphoreType.DMA,
        ],
        compiler_params=pltpu.CompilerParams(vmem_limit_bytes=24 << 20),
        name="filterbank" if pieces else "transform",
    )(chan, volts, *args)


def order_kernel(pieces, *refs):
    place, out, turned = refs[pieces:]
    half = refs[0].shape[1] // 2
    slots = refs[0].shape[0]
    parts = []
    for part in range(2):
        rows = jnp.concatenate([refs[d][:, part * half : (part + 1) * half] for d in range(pieces)], axis=1)
        got = jnp.dot(rows, place[...], preferred_element_type=f32)
        parts.append(got.reshape(slots // COARSE, 1, COARSE, got.shape[1]))
    re, im = parts
    shape = (2 * slots, re.shape[3])
    out[...] = jnp.concatenate([re, im], axis=1).reshape(shape).astype(bf16)
    turned[...] = jnp.concatenate([im, -re], axis=1).reshape(shape).astype(bf16)


def order(blocks, place):
    slots = blocks[0].shape[0]
    vmem = pl.BlockSpec(memory_space=pltpu.VMEM)
    shape = jax.ShapeDtypeStruct((2 * slots, place.shape[1]), bf16)
    return pl.pallas_call(
        functools.partial(order_kernel, len(blocks)),
        out_shape=[shape, shape],
        in_specs=[vmem] * (len(blocks) + 1),
        out_specs=[vmem] * 2,
        compiler_params=pltpu.CompilerParams(vmem_limit_bytes=16 << 20),
        name="order",
    )(*blocks, place)


def gram_kernel(frames, start, scale, pol_ref, own, turned, other, *refs):
    out, ring, sems = refs[-3:]
    stations = own.shape[1] // frames
    tiles = stations // LANES
    first = pol_ref[0] == 0
    turns = (((0,), (0,)), ((), ()))
    count = own.shape[0] // (2 * COARSE)
    depth = ring.shape[0]

    def copies(j):
        slot = lax.rem(j, depth)
        return [
            pltpu.make_async_copy(ring.at[slot, part], out.at[part, start + j], sems.at[slot, part])
            for part in range(2)
        ]

    def one(j, carry):
        slot = lax.rem(j, depth)

        @pl.when(j >= depth)
        def _():
            for copy in copies(j - depth):
                copy.wait()

        def stack(ref):
            rows = pl.ds(pl.multiple_of(2 * COARSE * j, 2 * COARSE), 2 * COARSE)
            return jnp.concatenate([ref[rows, f * stations : (f + 1) * stations] for f in range(frames)], axis=0)

        mine, mine_turned, theirs = stack(own), stack(turned), stack(other)
        right = jnp.concatenate([jnp.where(first, mine, theirs), jnp.where(first, theirs, mine)], axis=1)
        for part, left in enumerate((mine, mine_turned)):
            got = lax.dot_general(left, right, turns, preferred_element_type=f32) * scale
            for q in range(2):
                for t in range(tiles):
                    at = q * stations + t * LANES
                    ring[slot, part, pl.ds(2 * t + q, stations, stride=2 * tiles), :] = got[:, at : at + LANES]
        for copy in copies(j):
            copy.start()
        return carry

    lax.fori_loop(0, count, one, 0)
    for j in range(count - depth, count):
        for copy in copies(j):
            copy.wait()


def gram(pol, own, turned, other, frames, coarse, start, into):
    count = own.shape[0] // (2 * COARSE)
    stations = own.shape[1] // frames
    rows = stations * 2 * (stations // LANES)
    depth = min(4, count)
    vmem, hbm = pl.BlockSpec(memory_space=pltpu.VMEM), pl.BlockSpec(memory_space=pltpu.HBM)
    more = [] if into is None else [into]
    return pl.pallas_call(
        functools.partial(gram_kernel, frames, start, 1.0 / (frames * COARSE)),
        out_shape=jax.ShapeDtypeStruct((2, coarse, rows, LANES), f32),
        in_specs=[pl.BlockSpec(memory_space=pltpu.SMEM), vmem, vmem, vmem] + [hbm] * len(more),
        out_specs=hbm,
        scratch_shapes=[pltpu.VMEM((depth, 2, rows, LANES), f32), pltpu.SemaphoreType.DMA((depth, 2))],
        input_output_aliases={4: 0} if more else {},
        compiler_params=pltpu.CompilerParams(vmem_limit_bytes=16 << 20),
        name="gram",
    )(pol, own, turned, other, *more)


def rolled(array, axis, start, size):
    return lax.dynamic_slice_in_dim(jnp.concatenate([array, array], axis=axis), start, size, axis=axis)


def groups_of(rows):
    half = rows // 2
    return [(0, half), (half, half)] if half % 16 == 0 else [(0, rows)]


def fast_body(voltages, fir_coeffs, flags, station_slot, chan_map):
    chans, stns = lax.axis_size("chan"), lax.axis_size("stn")
    chan, stn, pol = lax.axis_index("chan"), lax.axis_index("stn"), lax.axis_index("pol")
    here = voltages.shape[1]
    stations = station_slot.shape[0]
    frames = chans
    rows = here // chans
    owners = chans * stns
    slots = CH // owners
    coarse = slots // COARSE
    groups = groups_of(rows)
    shares = voltages.reshape(chans, rows, FL)
    blocks = []
    for offset, size in groups:
        blocks.append([])
        for d in range(1, chans):
            share = lax.dynamic_index_in_dim(shares[:, offset : offset + size], chan ^ d, 0, keepdims=False)
            blocks[-1].append(lax.ppermute(share, "chan", [(i, i ^ d) for i in range(chans)]))
    lane_of = (chan_map % RAD) * HALF + chan_map // RAD
    lane_of = rolled(rolled(lane_of.reshape(chans, stns, slots), 0, chan, chans), 1, stn, stns)
    select = onehot(lane_of.reshape(CH), jnp.arange(CH, dtype=jnp.int32))
    dist = jnp.arange(owners, dtype=jnp.int32)
    row0 = (stn - dist % stns) % stns * here + (chan - dist // stns) % chans * rows
    col = station_slot[None, :] + stations * jnp.arange(frames, dtype=jnp.int32)[:, None]
    prior, place = [], []
    for n, (group, block) in enumerate(zip(groups, blocks, strict=True)):
        count = owners if n == len(groups) - 1 else 0
        pieces = filterbank(
            chan.reshape(1), voltages, block, fir_coeffs, flags, rows, group, prior, select, count
        )
        prior = [pieces]
        row = row0[:, None, None] + group[0] + jnp.arange(group[1], dtype=jnp.int32)[None, None, :]
        row = row + stations * jnp.arange(frames, dtype=jnp.int32)[None, :, None]
        place.append(row.reshape(owners, -1))
    place = onehot(jnp.concatenate(place, axis=1).reshape(-1), col.reshape(-1))
    got = [pieces[0]]
    for d in range(1, owners):
        dc, ds = divmod(d, stns)
        route = [(i * stns + j, (i + dc) % chans * stns + (j + ds) % stns) for i in range(chans) for j in range(stns)]
        got.append(lax.ppermute(pieces[d], ("chan", "stn"), route))
    own, turned = order(got, place)
    other = lax.ppermute(own, "pol", [(0, 1), (1, 0)])
    out = gram(pol.reshape(1), own, turned, other, frames, coarse, 0, None)
    tiles = stations // LANES
    out = out.reshape(2, -1, stations, tiles, 2, LANES).transpose(0, 1, 2, 4, 3, 5)
    return out.reshape(2, -1, 1, stations, 2, stations)


def general_body(voltages, fir_coeffs, flags, station_slot, chan_map):
    high = lax.Precision.HIGHEST
    here = voltages.shape[1]
    chans, stns = lax.axis_size("chan"), lax.axis_size("stn")
    frames_here = voltages.shape[2] // FL
    frames = voltages.reshape(here, frames_here, FL)
    history = []
    for distance in range(1, (TAPS - 1 + frames_here - 1) // frames_here + 1):
        route = [(i - distance, i) for i in range(distance, chans)]
        history = [lax.ppermute(frames, "chan", route)] + history
    window = jnp.concatenate(history + [frames], axis=1)
    window = window[:, window.shape[1] - frames_here - TAPS + 1 :]
    filtered = jnp.zeros((here, frames_here, FL), f32)
    for tap in range(TAPS):
        filtered = filtered + fir_coeffs[tap][None, None, :] * window[:, tap : tap + frames_here, :].astype(f32)
    side = math.isqrt(FL)

    def angles(rows, cols, period):
        product = jnp.arange(rows, dtype=jnp.int32)[:, None] * jnp.arange(cols, dtype=jnp.int32)[None, :]
        phase = (product % period).astype(f32) * (2.0 * math.pi / period)
        return jnp.cos(phase), jnp.sin(phase)

    grid = filtered.reshape(here, frames_here, side, side)
    cos, sin = angles(side, side, side)
    re = jnp.einsum("sfqp,qc->sfpc", grid, cos, precision=high)
    im = -jnp.einsum("sfqp,qc->sfpc", grid, sin, precision=high)
    cos, sin = angles(side, side, FL)
    re, im = re * cos + im * sin, im * cos - re * sin
    cos, sin = angles(side, side // 2, side)
    form = "sfpc,pk->kcfs"
    out_re = jnp.einsum(form, re, cos, precision=high) + jnp.einsum(form, im, sin, precision=high)
    out_im = jnp.einsum(form, im, cos, precision=high) - jnp.einsum(form, re, sin, precision=high)
    weight = jnp.tile(flags[0].astype(f32), frames_here) * FL**-0.5
    shape = (CH, 1, frames_here * here)
    spectra = jnp.concatenate(
        [(out_re.reshape(shape) * weight).astype(bf16), (out_im.reshape(shape) * weight).astype(bf16)], axis=1
    )
    select = onehot(chan_map, jnp.arange(CH, dtype=jnp.int32))
    spectra = jnp.einsum("sc,cpn->spn", select, spectra, preferred_element_type=f32).astype(bf16)
    pieces = lax.all_to_all(spectra, ("chan", "stn"), split_axis=0, concat_axis=2, tiled=True)
    pieces = pieces.reshape(-1, 2, chans, stns, frames_here, here).transpose(0, 1, 3, 5, 2, 4)
    total = chans * frames_here
    pieces = pieces.reshape(-1, COARSE, 2, stns * here, total)
    place = onehot(station_slot, jnp.arange(stns * here, dtype=jnp.int32))
    own = jnp.einsum("ar,jkprf->jkpaf", place, pieces, preferred_element_type=f32).astype(bf16)
    both = lax.all_gather(own[None], "pol", axis=0, tiled=True)
    form = "jkrf,qjksf->jrqs"

    def dot(left, right):
        return jnp.einsum(form, left, right, preferred_element_type=f32)

    own_re, own_im, re, im = own[:, :, 0], own[:, :, 1], both[:, :, :, 0], both[:, :, :, 1]
    block = jnp.stack([dot(own_re, re) + dot(own_im, im), dot(own_im, re) - dot(own_re, im)], axis=0)
    return (block * (1.0 / (total * COARSE)))[:, :, None]


def body(voltages, fir_coeffs, flags, station_slot, chan_map):
    chans, stns = lax.axis_size("chan"), lax.axis_size("stn")
    here, stations = voltages.shape[1], station_slot.shape[0]
    fits = (
        voltages.shape[2] == FL
        and chans <= TAPS
        and chans & (chans - 1) == 0
        and here % chans == 0
        and here // chans % 16 == 0
        and here == LANES
        and stations % LANES == 0
        and CH // (chans * stns) % 16 == 0
    )
    return (fast_body if fits else general_body)(voltages, fir_coeffs, flags, station_slot, chan_map)


def solution(mesh):
    in_specs = (P(("grp", "pol"), "stn", "chan"), P(), P(("grp", "pol"), "stn"), P(), P())
    out_specs = P("grp", ("chan", "stn"), "pol", None, None, None)
    return jax.shard_map(body, mesh=mesh, in_specs=in_specs, out_specs=out_specs, check_vma=False)
```

```python
import functools
import math

import jax
import jax.numpy as jnp
import numpy as np
from jax import lax
from jax.experimental import pallas as pl
from jax.experimental.pallas import tpu as pltpu
from jax.sharding import PartitionSpec as P

TAPS = 16
FL = 4096
CH = 2048
COARSE = 8
RAD = 16
PT = FL // RAD
HALF = PT // 2
LANES = 128
BATCH = 4

f32 = jnp.float32
bf16 = jnp.bfloat16


def onehot(rows, cols):
    return (rows[:, None] == cols[None, :]).astype(bf16)


@functools.cache
def tables():
    p = np.arange(PT)[None, :]
    rows = []
    for k2 in (np.arange(HALF), PT - 1 - np.arange(HALF)):
        phase = (k2[:, None] * p % PT) * (2.0 * math.pi / PT)
        rows += [np.cos(phase), -np.sin(phase)]
    table = np.concatenate(rows) * FL**-0.5
    high = table.astype(np.float32).astype(jnp.bfloat16)
    low = (table - high.astype(np.float64)).astype(np.float32).astype(jnp.bfloat16)
    phase = np.arange(1, RAD // 2 + 1)[:, None] * p * (2.0 * math.pi / FL)
    twiddle = np.concatenate([np.cos(phase), np.sin(phase)]).astype(np.float32)
    return high, low, twiddle


def real_dft16(x):
    def dft4(a0, a1, a2, a3):
        s02, d02, s13, d13 = a0 + a2, a0 - a2, a1 + a3, a1 - a3
        return s02 + s13, d02, -d13, s02 - s13

    cols = [dft4(x[b], x[4 + b], x[8 + b], x[12 + b]) for b in range(4)]
    out = [None] * 9
    r0, r1, i1, r2 = dft4(*(cols[b][0] for b in range(4)))
    out[0], out[4], out[8] = (r0, None), (r1, i1), (r2, None)
    h = math.sqrt(0.5)
    v0, v1, v2, v3 = (cols[b][3] for b in range(4))
    pr, pi = h * (v1 - v3), -h * (v1 + v3)
    out[2] = (v0 + pr, pi - v2)
    out[6] = (v0 - pr, v2 + pi)
    c1, s1 = math.cos(math.pi / 8), math.sin(math.pi / 8)
    re0, im0 = cols[0][1], cols[0][2]
    re1 = cols[1][1] * c1 + cols[1][2] * s1
    im1 = cols[1][2] * c1 - cols[1][1] * s1
    re2 = (cols[2][1] + cols[2][2]) * h
    im2 = (cols[2][2] - cols[2][1]) * h
    re3 = cols[3][1] * s1 + cols[3][2] * c1
    im3 = cols[3][2] * s1 - cols[3][1] * c1
    ar, ai, br, bi = re0 + re2, im0 + im2, re0 - re2, im0 - im2
    cr, ci, dr, di = re1 + re3, im1 + im3, re1 - re3, im1 - im3
    out[1] = (ar + cr, ai + ci)
    out[5] = (br + di, bi - dr)
    out[7] = (ar - cr, ci - ai)
    out[3] = (br - di, -bi - dr)
    return out


def split(value):
    high = value.astype(bf16)
    return high, (value - high.astype(f32)).astype(bf16)


def filterbank_kernel(frames, share, group, pieces, before, chan_ref, *refs):
    offset, rows = group
    volts, *blocks = refs[:frames]
    blocks = blocks[::-1]
    fir, flag, twiddle, dft_hi, dft_lo, *rest = refs[frames:-4]
    x, u_hi, u_lo, sem = refs[-4:]
    if pieces:
        spec = rest.pop()
    prior = [rest.pop(0) for _ in range(before)]
    select, *outs = rest
    if not pieces:
        [spec] = outs
    total = frames * rows
    whole = frames * share
    chan = chan_ref[0]
    begin = pl.multiple_of(chan * share + offset, rows)
    load = pltpu.make_async_copy(volts.at[0, pl.ds(begin, rows)], x.at[chan], sem)
    load.start()
    for d in range(1, frames):
        x[jnp.bitwise_xor(chan, d)] = blocks[d - 1][...]
    for earlier in prior:
        spec[...] = earlier[...]
    load.wait()
    step = 16
    halves = PT // LANES
    for f in range(frames):

        def unit(i, carry, f=f):
            at = pl.multiple_of(i // halves * step, step)
            base = pl.multiple_of(i % halves * LANES, LANES)
            filtered = []
            for q in range(RAD):
                lanes = pl.ds(pl.multiple_of(PT * q + base, LANES), LANES)
                acc = None
                for lag in range(f + 1):
                    tap = TAPS - 1 - lag
                    term = fir[tap : tap + 1, lanes] * x[f - lag, pl.ds(at, step), lanes].astype(f32)
                    acc = term if acc is None else acc + term
                filtered.append(acc)
            parts = []
            for c, (re, im) in enumerate(real_dft16(filtered)):
                if c == 0:
                    parts.append(re)
                    continue
                cos = twiddle[c - 1 : c, pl.ds(base, LANES)]
                sin = twiddle[RAD // 2 + c - 1 : RAD // 2 + c, pl.ds(base, LANES)]
                parts += [re * cos, -re * sin] if im is None else [re * cos + im * sin, im * cos - re * sin]
            for n, part in enumerate(parts):
                high, low = split(part)
                to = (n, pl.ds(pl.multiple_of(f * rows + at, step), step), pl.ds(base, LANES))
                u_hi[to] = high
                u_lo[to] = low
            return carry

        lax.fori_loop(0, rows // step * halves, unit, 0)
    contract = (((1,), (1,)), ((), ()))

    def three(at, count, outputs):
        a = u_hi[pl.ds(at, count)].reshape(count * total, PT)
        b = u_lo[pl.ds(at, count)].reshape(count * total, PT)
        hi, lo = dft_hi[:outputs], dft_lo[:outputs]
        out = lax.dot_general(hi, a, contract, preferred_element_type=f32)
        out = out + lax.dot_general(hi, b, contract, preferred_element_type=f32)
        return out + lax.dot_general(lo, a, contract, preferred_element_type=f32)

    lane = lax.broadcasted_iota(jnp.int32, (1, flag.shape[1]), 1)
    mine = pltpu.roll(flag[...].astype(f32), lax.rem(2 * flag.shape[1] - begin, flag.shape[1]), 1)
    keep = mine
    for f in range(1, frames):
        keep = jnp.where(lane >= f * rows, pltpu.roll(mine, f * rows, 1), keep)
    keep = keep[:, :total]
    lanes_of = [slice(part * whole + frames * offset, part * whole + frames * offset + total) for part in range(2)]

    def put(c, re, im):
        spec[c, :, lanes_of[0]] = (re * keep).astype(bf16)
        spec[c, :, lanes_of[1]] = (im * keep).astype(bf16)

    got = three(0, 1, PT)
    put(0, got[:HALF], got[HALF:])
    per = max(1, LANES // total)
    o = PT + HALF
    for first in range(1, RAD // 2 + 1, per):
        got = three(2 * first - 1, 2 * per, PT if first == RAD // 2 else 2 * PT)
        for k in range(per):
            c = first + k
            re, im = got[:, 2 * k * total : (2 * k + 1) * total], got[:, (2 * k + 1) * total : (2 * k + 2) * total]
            put(c, re[:HALF] - im[HALF:PT], re[HALF:PT] + im[:HALF])
            if c < RAD // 2:
                put(RAD - c, re[PT:o] - im[o:], -(re[o:] + im[PT:o]))
    if not pieces:
        return
    right = spec[...].reshape(CH, 2 * whole)
    size = CH // pieces
    for first in range(0, pieces, BATCH):
        got = jnp.dot(select[first * size : (first + BATCH) * size], right, preferred_element_type=f32).astype(bf16)
        for d in range(BATCH):
            outs[first + d][...] = got[d * size : (d + 1) * size]


def filterbank(chan, volts, blocks, fir, flag, share, group, prior, select, pieces):
    frames, rows = len(blocks) + 1, group[1]
    total, whole = frames * rows, frames * share
    vmem = pl.BlockSpec(memory_space=pltpu.VMEM)
    high, low, twiddle = (jnp.asarray(t) for t in tables())
    spec = (RAD, HALF, 2 * whole)
    args = [*blocks[::-1], fir, flag, twiddle, high, low] + prior + [select]
    outs = [jax.ShapeDtypeStruct((CH // pieces, 2 * whole), bf16)] * pieces if pieces else jax.ShapeDtypeStruct(spec, bf16)
    return pl.pallas_call(
        functools.partial(filterbank_kernel, frames, share, group, pieces, len(prior)),
        out_shape=outs,
        in_specs=[pl.BlockSpec(memory_space=pltpu.SMEM), pl.BlockSpec(memory_space=pl.ANY)] + [vmem] * len(args),
        out_specs=[vmem] * pieces if pieces else vmem,
        scratch_shapes=([pltpu.VMEM(spec, bf16)] if pieces else [])
        + [
            pltpu.VMEM((frames, rows, FL), bf16),
            pltpu.VMEM((RAD + 1, total, PT), bf16),
            pltpu.VMEM((RAD + 1, total, PT), bf16),
            pltpu.SemaphoreType.DMA,
        ],
        compiler_params=pltpu.CompilerParams(vmem_limit_bytes=24 << 20),
        name="filterbank" if pieces else "transform",
    )(chan, volts, *args)


def order_kernel(pieces, *refs):
    place, out, turned = refs[pieces:]
    half = refs[0].shape[1] // 2
    slots = refs[0].shape[0]
    parts = []
    for part in range(2):
        rows = jnp.concatenate([refs[d][:, part * half : (part + 1) * half] for d in range(pieces)], axis=1)
        got = jnp.dot(rows, place[...], preferred_element_type=f32)
        parts.append(got.reshape(slots // COARSE, 1, COARSE, got.shape[1]))
    re, im = parts
    shape = (2 * slots, re.shape[3])
    out[...] = jnp.concatenate([re, im], axis=1).reshape(shape).astype(bf16)
    turned[...] = jnp.concatenate([im, -re], axis=1).reshape(shape).astype(bf16)


def order(blocks, place):
    slots = blocks[0].shape[0]
    vmem = pl.BlockSpec(memory_space=pltpu.VMEM)
    shape = jax.ShapeDtypeStruct((2 * slots, place.shape[1]), bf16)
    return pl.pallas_call(
        functools.partial(order_kernel, len(blocks)),
        out_shape=[shape, shape],
        in_specs=[vmem] * (len(blocks) + 1),
        out_specs=[vmem] * 2,
        compiler_params=pltpu.CompilerParams(vmem_limit_bytes=16 << 20),
        name="order",
    )(*blocks, place)


def gram_kernel(frames, start, scale, pol_ref, own, turned, other, *refs):
    out, ring, sems = refs[-3:]
    stations = own.shape[1] // frames
    tiles = stations // LANES
    first = pol_ref[0] == 0
    turns = (((0,), (0,)), ((), ()))
    count = own.shape[0] // (2 * COARSE)
    depth = ring.shape[0]

    def copies(j):
        slot = lax.rem(j, depth)
        return [
            pltpu.make_async_copy(ring.at[slot, part], out.at[part, start + j], sems.at[slot, part])
            for part in range(2)
        ]

    def one(j, carry):
        slot = lax.rem(j, depth)

        @pl.when(j >= depth)
        def _():
            for copy in copies(j - depth):
                copy.wait()

        def stack(ref):
            rows = pl.ds(pl.multiple_of(2 * COARSE * j, 2 * COARSE), 2 * COARSE)
            return jnp.concatenate([ref[rows, f * stations : (f + 1) * stations] for f in range(frames)], axis=0)

        mine, mine_turned, theirs = stack(own), stack(turned), stack(other)
        right = jnp.concatenate([jnp.where(first, mine, theirs), jnp.where(first, theirs, mine)], axis=1)
        for part, left in enumerate((mine, mine_turned)):
            got = lax.dot_general(left, right, turns, preferred_element_type=f32) * scale
            for q in range(2):
                for t in range(tiles):
                    at = q * stations + t * LANES
                    ring[slot, part, pl.ds(2 * t + q, stations, stride=2 * tiles), :] = got[:, at : at + LANES]
        for copy in copies(j):
            copy.start()
        return carry

    lax.fori_loop(0, count, one, 0)
    for j in range(count - depth, count):
        for copy in copies(j):
            copy.wait()


def gram(pol, own, turned, other, frames, coarse, start, into):
    count = own.shape[0] // (2 * COARSE)
    stations = own.shape[1] // frames
    rows = stations * 2 * (stations // LANES)
    depth = min(4, count)
    vmem, hbm = pl.BlockSpec(memory_space=pltpu.VMEM), pl.BlockSpec(memory_space=pltpu.HBM)
    more = [] if into is None else [into]
    return pl.pallas_call(
        functools.partial(gram_kernel, frames, start, 1.0 / (frames * COARSE)),
        out_shape=jax.ShapeDtypeStruct((2, coarse, rows, LANES), f32),
        in_specs=[pl.BlockSpec(memory_space=pltpu.SMEM), vmem, vmem, vmem] + [hbm] * len(more),
        out_specs=hbm,
        scratch_shapes=[pltpu.VMEM((depth, 2, rows, LANES), f32), pltpu.SemaphoreType.DMA((depth, 2))],
        input_output_aliases={4: 0} if more else {},
        compiler_params=pltpu.CompilerParams(vmem_limit_bytes=16 << 20),
        name="gram",
    )(pol, own, turned, other, *more)


def rolled(array, axis, start, size):
    return lax.dynamic_slice_in_dim(jnp.concatenate([array, array], axis=axis), start, size, axis=axis)


def groups_of(rows):
    half = rows // 2
    return [(0, half), (half, half)] if half % 16 == 0 else [(0, rows)]


def fast_body(voltages, fir_coeffs, flags, station_slot, chan_map):
    chans, stns = lax.axis_size("chan"), lax.axis_size("stn")
    chan, stn, pol = lax.axis_index("chan"), lax.axis_index("stn"), lax.axis_index("pol")
    here = voltages.shape[1]
    stations = station_slot.shape[0]
    frames = chans
    rows = here // chans
    owners = chans * stns
    slots = CH // owners
    coarse = slots // COARSE
    groups = groups_of(rows)
    shares = voltages.reshape(chans, rows, FL)
    blocks = []
    for offset, size in groups:
        blocks.append([])
        for d in range(1, chans):
            share = lax.dynamic_index_in_dim(shares[:, offset : offset + size], chan ^ d, 0, keepdims=False)
            blocks[-1].append(lax.ppermute(share, "chan", [(i, i ^ d) for i in range(chans)]))
    lane_of = (chan_map % RAD) * HALF + chan_map // RAD
    lane_of = rolled(rolled(lane_of.reshape(chans, stns, slots), 0, chan, chans), 1, stn, stns)
    select = onehot(lane_of.reshape(CH), jnp.arange(CH, dtype=jnp.int32))
    far = [*range(stns, owners), *range(1, stns)]
    dist = jnp.asarray(np.array([0, *far], np.int32))
    row0 = (stn - dist % stns) % stns * here + (chan - dist // stns) % chans * rows
    col = station_slot[None, :] + stations * jnp.arange(frames, dtype=jnp.int32)[:, None]
    prior, place = [], []
    for n, (group, block) in enumerate(zip(groups, blocks, strict=True)):
        count = owners if n == len(groups) - 1 else 0
        pieces = filterbank(
            chan.reshape(1), voltages, block, fir_coeffs, flags, rows, group, prior, select, count
        )
        prior = [pieces]
        row = row0[:, None, None] + group[0] + jnp.arange(group[1], dtype=jnp.int32)[None, None, :]
        row = row + stations * jnp.arange(frames, dtype=jnp.int32)[None, :, None]
        place.append(row.reshape(owners, -1))
    place = onehot(jnp.concatenate(place, axis=1).reshape(-1), col.reshape(-1))
    got = [pieces[0]]
    for d in far:
        dc, ds = divmod(d, stns)
        route = [(i * stns + j, (i + dc) % chans * stns + (j + ds) % stns) for i in range(chans) for j in range(stns)]
        got.append(lax.ppermute(pieces[d], ("chan", "stn"), route))
    own, turned = order(got, place)
    other = lax.ppermute(own, "pol", [(0, 1), (1, 0)])
    out = gram(pol.reshape(1), own, turned, other, frames, coarse, 0, None)
    tiles = stations // LANES
    out = out.reshape(2, -1, stations, tiles, 2, LANES).transpose(0, 1, 2, 4, 3, 5)
    return out.reshape(2, -1, 1, stations, 2, stations)


def general_body(voltages, fir_coeffs, flags, station_slot, chan_map):
    high = lax.Precision.HIGHEST
    here = voltages.shape[1]
    chans, stns = lax.axis_size("chan"), lax.axis_size("stn")
    frames_here = voltages.shape[2] // FL
    frames = voltages.reshape(here, frames_here, FL)
    history = []
    for distance in range(1, (TAPS - 1 + frames_here - 1) // frames_here + 1):
        route = [(i - distance, i) for i in range(distance, chans)]
        history = [lax.ppermute(frames, "chan", route)] + history
    window = jnp.concatenate(history + [frames], axis=1)
    window = window[:, window.shape[1] - frames_here - TAPS + 1 :]
    filtered = jnp.zeros((here, frames_here, FL), f32)
    for tap in range(TAPS):
        filtered = filtered + fir_coeffs[tap][None, None, :] * window[:, tap : tap + frames_here, :].astype(f32)
    side = math.isqrt(FL)

    def angles(rows, cols, period):
        product = jnp.arange(rows, dtype=jnp.int32)[:, None] * jnp.arange(cols, dtype=jnp.int32)[None, :]
        phase = (product % period).astype(f32) * (2.0 * math.pi / period)
        return jnp.cos(phase), jnp.sin(phase)

    grid = filtered.reshape(here, frames_here, side, side)
    cos, sin = angles(side, side, side)
    re = jnp.einsum("sfqp,qc->sfpc", grid, cos, precision=high)
    im = -jnp.einsum("sfqp,qc->sfpc", grid, sin, precision=high)
    cos, sin = angles(side, side, FL)
    re, im = re * cos + im * sin, im * cos - re * sin
    cos, sin = angles(side, side // 2, side)
    form = "sfpc,pk->kcfs"
    out_re = jnp.einsum(form, re, cos, precision=high) + jnp.einsum(form, im, sin, precision=high)
    out_im = jnp.einsum(form, im, cos, precision=high) - jnp.einsum(form, re, sin, precision=high)
    weight = jnp.tile(flags[0].astype(f32), frames_here) * FL**-0.5
    shape = (CH, 1, frames_here * here)
    spectra = jnp.concatenate(
        [(out_re.reshape(shape) * weight).astype(bf16), (out_im.reshape(shape) * weight).astype(bf16)], axis=1
    )
    select = onehot(chan_map, jnp.arange(CH, dtype=jnp.int32))
    spectra = jnp.einsum("sc,cpn->spn", select, spectra, preferred_element_type=f32).astype(bf16)
    pieces = lax.all_to_all(spectra, ("chan", "stn"), split_axis=0, concat_axis=2, tiled=True)
    pieces = pieces.reshape(-1, 2, chans, stns, frames_here, here).transpose(0, 1, 3, 5, 2, 4)
    total = chans * frames_here
    pieces = pieces.reshape(-1, COARSE, 2, stns * here, total)
    place = onehot(station_slot, jnp.arange(stns * here, dtype=jnp.int32))
    own = jnp.einsum("ar,jkprf->jkpaf", place, pieces, preferred_element_type=f32).astype(bf16)
    both = lax.all_gather(own[None], "pol", axis=0, tiled=True)
    form = "jkrf,qjksf->jrqs"

    def dot(left, right):
        return jnp.einsum(form, left, right, preferred_element_type=f32)

    own_re, own_im, re, im = own[:, :, 0], own[:, :, 1], both[:, :, :, 0], both[:, :, :, 1]
    block = jnp.stack([dot(own_re, re) + dot(own_im, im), dot(own_im, re) - dot(own_re, im)], axis=0)
    return (block * (1.0 / (total * COARSE)))[:, :, None]


def body(voltages, fir_coeffs, flags, station_slot, chan_map):
    chans, stns = lax.axis_size("chan"), lax.axis_size("stn")
    here, stations = voltages.shape[1], station_slot.shape[0]
    fits = (
        voltages.shape[2] == FL
        and chans <= TAPS
        and chans & (chans - 1) == 0
        and here % chans == 0
        and here // chans % 16 == 0
        and here == LANES
        and stations % LANES == 0
        and CH // (chans * stns) % 16 == 0
    )
    return (fast_body if fits else general_body)(voltages, fir_coeffs, flags, station_slot, chan_map)


def solution(mesh):
    in_specs = (P(("grp", "pol"), "stn", "chan"), P(), P(("grp", "pol"), "stn"), P(), P())
    out_specs = P("grp", ("chan", "stn"), "pol", None, None, None)
    return jax.shard_map(body, mesh=mesh, in_specs=in_specs, out_specs=out_specs, check_vma=False)
```
